32 devices in a mesh: band: 4 (over z), dom: 8 (over y, x, core).
Axes of the slice: x: 2, y: 2, z: 4, core: 2. Of those that a mesh axis runs over, the one named last changes fastest.
Arguments:
- orbitals: float32 [64, 48, 48, 128], P('band', 'dom'), may hold values from -6 to 6
- occupation: float32 [64], P('band'), may hold values from 0.005 to 0.03
- dielectric: float32 [48, 48, 128], P('dom'), may hold values from 1 to 10
- core_density: float32 [48, 48, 128], P('dom'), may hold values from 0.05 to 0.5
- start_field: float32 [48, 48, 128], P('dom'), may hold values from -6 to 6
Outputs:
- potential: float32 [48, 48, 128], P('dom')
- filtered: float32 [64, 48, 48, 128], P('band', 'dom')
The draws below stay inside these ranges and needn't reach their ends.
All inputs are finite; a program needn't handle non-finite values.
Results may differ from the reference program's by a relative error of at most 0.00002.
Values sent between devices are 32-bit elements; how exact they have to be, the bound alone decides.
A program may use at most 64 MiB of HBM per device.

```python
import math
import jax
import jax.numpy as jnp
from jax import lax

NORB = 64
NY = 48
NZ = 128
ITERS = 4
DEGREE = 4
NX = 48


def level_of(rng, extent, cuts, smallest, largest):
    gain = 1.0
    for axis_at, parts in cuts:
        draws = jax.random.uniform(jax.random.fold_in(jax.random.fold_in(rng, 6), axis_at), (parts,), jnp.float32, smallest / len(cuts), largest / len(cuts))
        gain = gain * jnp.repeat(jnp.exp(draws), extent[axis_at] // parts).reshape((-1,) + (1,) * (len(extent) - 1 - axis_at))
    return gain


def centred(rng, dims, spread, limit, pieces=(), held_as=jnp.bfloat16):
    drawn = spread * jax.random.normal(rng, dims, jnp.float32)
    if pieces:
        drawn = drawn * level_of(rng, dims, pieces, -0.22, 0.18)
    return jnp.clip(drawn, -limit, limit).astype(held_as)


def setup_inputs(seed: int = 0) -> dict:
    key_list = jax.random.split(jax.random.key(seed), 6)
    return {
        "orbitals": centred(key_list[0], (NORB, NX, NY, NZ), 1.0, 6.0, ((0, 4), (1, 8)), jnp.float32),
        "occupation": jnp.clip(jnp.exp(math.log(0.03) - 1.7917595 * jax.random.uniform(key_list[1], (NORB,), jnp.float32) ** level_of(key_list[1], (NORB,), ((0, 4),), -0.2, 0.2)), 0.005, 0.03),
        "dielectric": jnp.clip(jnp.exp(math.log(10.0) - 2.3025851 * jax.random.uniform(key_list[2], (NX, NY, NZ), jnp.float32) ** level_of(key_list[2], (NX, NY, NZ), ((0, 8),), -0.2, 0.2)), 1.0, 10.0),
        "core_density": jnp.clip(jnp.exp(math.log(0.5) - 2.3025851 * jax.random.uniform(key_list[3], (NX, NY, NZ), jnp.float32) ** level_of(key_list[3], (NX, NY, NZ), ((0, 8),), -0.2, 0.2)), 0.05, 0.5),
        "start_field": centred(key_list[4], (NX, NY, NZ), 1.0, 6.0, ((0, 8),), jnp.float32),
    }


coeff_one = 1.5
coeff_two = -0.15
coeff_three = 1.0 / 90.0
coeff_zero = -49.0 / 18.0
center_value = 5.25
half_value = 4.75
slater = -0.98474502184269641


def laplace(padded):
    size_x = padded.shape[-3] - 6
    size_y = padded.shape[-2] - 6
    size_z = padded.shape[-1] - 6
    core = padded[..., 3:3 + size_x, 3:3 + size_y, 3:3 + size_z]
    total = 3.0 * coeff_zero * core
    for dist, weight in ((1, coeff_one), (2, coeff_two), (3, coeff_three)):
        along = padded[..., 3 + dist:3 + dist + size_x, 3:3 + size_y, 3:3 + size_z]
        along = along + padded[..., 3 - dist:3 - dist + size_x, 3:3 + size_y, 3:3 + size_z]
        along = along + padded[..., 3:3 + size_x, 3 + dist:3 + dist + size_y, 3:3 + size_z]
        along = along + padded[..., 3:3 + size_x, 3 - dist:3 - dist + size_y, 3:3 + size_z]
        along = along + padded[..., 3:3 + size_x, 3:3 + size_y, 3 + dist:3 + dist + size_z]
        along = along + padded[..., 3:3 + size_x, 3:3 + size_y, 3 - dist:3 - dist + size_z]
        total = total + weight * along
    return total


def face_weights(permit, padded):
    weights = (
        0.5 * (permit + padded[2:, 1:-1, 1:-1]),
        0.5 * (permit + padded[:-2, 1:-1, 1:-1]),
        0.5 * (permit + padded[1:-1, 2:, 1:-1]),
        0.5 * (permit + padded[1:-1, :-2, 1:-1]),
        0.5 * (permit + padded[1:-1, 1:-1, 2:]),
        0.5 * (permit + padded[1:-1, 1:-1, :-2]),
    )
    denominator = weights[0] + weights[1] + weights[2] + weights[3] + weights[4] + weights[5]
    return weights, denominator


def sweep(padded, weights, denominator, source):
    numerator = weights[0] * padded[2:, 1:-1, 1:-1] + weights[1] * padded[:-2, 1:-1, 1:-1]
    numerator = numerator + weights[2] * padded[1:-1, 2:, 1:-1] + weights[3] * padded[1:-1, :-2, 1:-1]
    numerator = numerator + weights[4] * padded[1:-1, 1:-1, 2:] + weights[5] * padded[1:-1, 1:-1, :-2]
    return (numerator + source) / denominator


def reference(orbitals, occupation, dielectric, core_density, start_field):
    density = jnp.sum(occupation[:, None, None, None] * orbitals * orbitals, axis=0)
    weights, denominator = face_weights(dielectric, jnp.pad(dielectric, 1))
    source = 4.0 * density
    field = start_field
    for turn_index in range(ITERS):
        field = sweep(jnp.pad(field, 1), weights, denominator, source)
    potential = field + slater * jnp.cbrt(density + core_density)

    def hamil(block):
        return -0.5 * laplace(jnp.pad(block, 3)) + potential * block

    def one_orbital(orbital):
        before = orbital
        current = (hamil(orbital) - center_value * orbital) / half_value
        for turn_index in range(DEGREE - 1):
            nextone = 2.0 * (hamil(current) - center_value * current) / half_value - before
            before = current
            current = nextone
        return current

    filtered = lax.map(one_orbital, orbitals)
    return potential, filtered
```

```python
import functools

import jax
import jax.numpy as jnp
from jax import lax
from jax.experimental import pallas as pl
from jax.experimental.pallas import tpu as pltpu
from jax.sharding import PartitionSpec as P

ITERS = 4
DEGREE = 4


coeff_one = 1.5
coeff_two = -0.15
coeff_three = 1.0 / 90.0
coeff_zero = -49.0 / 18.0
center_value = 5.25
half_value = 4.75
slater = -0.9847450218426964


def padded_2(cells, sides, width):
    for axis, dim in sides:
        count = lax.axis_size(axis)
        ends = count - 1
        head = lax.slice_in_dim(cells, 0, width, axis=dim)
        tail = lax.slice_in_dim(cells, cells.shape[dim] - width, cells.shape[dim], axis=dim)
        cells = jnp.concatenate(
            [
                lax.ppermute(tail, axis, [(i, (i + 1) % count) for i in range(ends)]),
                cells,
                lax.ppermute(head, axis, [((i + 1) % count, i) for i in range(ends)]),
            ],
            axis=dim,
        )
    return cells


def laplace(padded):
    size_x = padded.shape[-3] - 6
    size_y = padded.shape[-2] - 6
    size_z = padded.shape[-1] - 6
    core = padded[..., 3 : 3 + size_x, 3 : 3 + size_y, 3 : 3 + size_z]
    total = 3.0 * coeff_zero * core
    for dist, weight in ((1, coeff_one), (2, coeff_two), (3, coeff_three)):
        along = padded[..., 3 + dist : 3 + dist + size_x, 3 : 3 + size_y, 3 : 3 + size_z]
        along = along + padded[..., 3 - dist : 3 - dist + size_x, 3 : 3 + size_y, 3 : 3 + size_z]
        along = along + padded[..., 3 : 3 + size_x, 3 + dist : 3 + dist + size_y, 3 : 3 + size_z]
        along = along + padded[..., 3 : 3 + size_x, 3 - dist : 3 - dist + size_y, 3 : 3 + size_z]
        along = along + padded[..., 3 : 3 + size_x, 3 : 3 + size_y, 3 + dist : 3 + dist + size_z]
        along = along + padded[..., 3 : 3 + size_x, 3 : 3 + size_y, 3 - dist : 3 - dist + size_z]
        total = total + weight * along
    return total


def face_weights(permit, padded):
    weights = (
        0.5 * (permit + padded[2:, 1:-1, 1:-1]),
        0.5 * (permit + padded[:-2, 1:-1, 1:-1]),
        0.5 * (permit + padded[1:-1, 2:, 1:-1]),
        0.5 * (permit + padded[1:-1, :-2, 1:-1]),
        0.5 * (permit + padded[1:-1, 1:-1, 2:]),
        0.5 * (permit + padded[1:-1, 1:-1, :-2]),
    )
    denominator = weights[0] + weights[1] + weights[2] + weights[3] + weights[4] + weights[5]
    return (weights, denominator)


def sweep(padded, weights, denominator, source):
    numerator = weights[0] * padded[2:, 1:-1, 1:-1] + weights[1] * padded[:-2, 1:-1, 1:-1]
    numerator = (
        numerator + weights[2] * padded[1:-1, 2:, 1:-1] + weights[3] * padded[1:-1, :-2, 1:-1]
    )
    numerator = (
        numerator + weights[4] * padded[1:-1, 1:-1, 2:] + weights[5] * padded[1:-1, 1:-1, :-2]
    )
    return (numerator + source) / denominator


def copies_rim(block):
    padded = padded_2(block, (("dom", 0),), 1)
    return jnp.pad(padded, ((0, 0), (1, 1), (1, 1)))


def apply_extended(padded_x, pot):
    padded = jnp.pad(padded_x, ((0, 0), (0, 0), (3, 3), (3, 3)))
    inner = padded_x[:, 3:-3]
    return -0.5 * laplace(padded) + pot[None] * inner


def local(orbitals, occupation, dielectric, core_density, start_field):
    partial_density = jnp.sum(occupation[:, None, None, None] * orbitals * orbitals, axis=0)
    density = lax.psum(partial_density, "band")
    permit_pad = padded_2(dielectric, (("dom", 0),), 1)
    permit_pad = jnp.pad(permit_pad, ((0, 0), (1, 1), (1, 1)))
    weights, denominator = face_weights(dielectric, permit_pad)
    source = 4.0 * density
    field = start_field
    for turn_index in range(ITERS):
        field = sweep(copies_rim(field), weights, denominator, source)
    potential = field + slater * jnp.cbrt(density + core_density)

    def hamil(block):
        padded = padded_2(block, (("dom", 1),), 3)
        return apply_extended(padded, potential)

    before = orbitals
    current = (hamil(orbitals) - center_value * orbitals) / half_value
    for turn_index in range(DEGREE - 1):
        nextone = 2.0 * (hamil(current) - center_value * current) / half_value - before
        before = current
        current = nextone
    return (potential, current)


MESH = pl.DeviceIdType.MESH
FEEDS = (5, 7, 7)


def exchange(count_band, count_dom, refs_in, potential_ref, filtered_ref, scratch):
    orbitals_ref, occupation_ref, dielectric_ref, core_ref, start_ref = refs_in
    (
        orbs, share, own, part_in, side, other, acc, density, eps, fields, weights, inverse,
        core, pot_own, strength, wave, wave_next, result, stripes, sums,
        load_sem, share_sem, halo_send, halo_recv, in_send, in_recv, acc_send, acc_recv,
        side_send, side_recv, other_send, other_recv, relay_send,
        den_send, den_recv, pot_send, pot_recv, swap_send, swap_recv, pass_send, pass_recv, out_send, out_recv, end_sem,
    ) = scratch
    norb, planes, rows, lanes = orbitals_ref.shape
    per = norb // count_dom
    wide = 8
    reach = 3
    band = lax.axis_index("band")
    dom = lax.axis_index("dom")
    middle = count_band // 2
    in_left = band < middle
    toward = jnp.where(in_left, 1, -1)
    inner = band + toward
    outer = band - toward
    has_outer = jnp.logical_and(band > 0, band < count_band - 1)
    is_mid = jnp.logical_or(band == middle - 1, band == middle)
    has_left = dom > 0
    has_right = dom < count_dom - 1
    partner = dom + 1 - 2 * lax.rem(dom, 2)
    body = pl.ds(wide, rows)

    def peer(step):
        return lax.rem(dom + step, count_dom)

    def remote(src, dst, send, recv, **where):
        return pltpu.make_async_remote_copy(
            src_ref=src, dst_ref=dst, send_sem=send, recv_sem=recv, device_id=where, device_id_type=MESH
        )

    loads = [
        pltpu.make_async_copy(orbitals_ref, orbs, load_sem.at[0]),
        pltpu.make_async_copy(dielectric_ref, eps.at[pl.ds(ITERS, planes), body], load_sem.at[1]),
        pltpu.make_async_copy(start_ref, fields.at[0, pl.ds(ITERS, planes), body], load_sem.at[2]),
        pltpu.make_async_copy(core_ref, core, load_sem.at[3]),
    ]
    for index in range(per):
        loads.append(
            pltpu.make_async_copy(
                orbitals_ref.at[dom * per + index],
                wave.at[index, pl.ds(reach + dom * planes, planes), body],
                load_sem.at[4 + index],
            )
        )
    shares = pltpu.make_async_copy(occupation_ref, share, share_sem.at[0])
    shares.start()
    for copy in loads:
        copy.start()

    barrier = pltpu.get_barrier_semaphore()
    for step in range(1, count_dom):
        pl.semaphore_signal(barrier, inc=1, device_id={"dom": peer(step)}, device_id_type=MESH)
    pl.semaphore_signal(barrier, inc=1, device_id={"band": inner}, device_id_type=MESH)
    pl.semaphore_signal(barrier, inc=1, device_id={"band": band + 1 - 2 * lax.rem(band, 2)}, device_id_type=MESH)

    @pl.when(has_outer)
    def _():
        pl.semaphore_signal(barrier, inc=1, device_id={"band": outer}, device_id_type=MESH)

    def clear_rows(ref, index):
        ref[index, :wide, :] = jnp.zeros((wide, lanes), jnp.float32)
        ref[index, wide + rows :, :] = jnp.zeros((wide, lanes), jnp.float32)

    def clear_plane(ref, index):
        ref[index] = jnp.zeros(ref.shape[1:], jnp.float32)

    extent = planes + 2 * ITERS

    @pl.loop(0, extent)
    def _(index):
        clear_rows(eps, index)
        for turn in range(ITERS):
            clear_rows(fields.at[turn], index)

    @pl.when(jnp.logical_not(has_left))
    def _():
        for index in range(ITERS):
            eps[index, body, :] = jnp.zeros((rows, lanes), jnp.float32)
            fields[0, index, body, :] = jnp.zeros((rows, lanes), jnp.float32)
        for index in range(ITERS - 1):
            density[index] = jnp.zeros((rows, lanes), jnp.float32)

    @pl.when(jnp.logical_not(has_right))
    def _():
        for index in range(ITERS):
            eps[ITERS + planes + index, body, :] = jnp.zeros((rows, lanes), jnp.float32)
            fields[0, ITERS + planes + index, body, :] = jnp.zeros((rows, lanes), jnp.float32)
        for index in range(ITERS - 1):
            density[ITERS - 1 + planes + index] = jnp.zeros((rows, lanes), jnp.float32)

    tall = count_dom * planes
    for ref in [stack.at[index] for stack in (wave, wave_next) for index in range(per)]:
        for index in range(reach):
            clear_plane(ref, index)
            clear_plane(ref, reach + tall + index)

        @pl.loop(reach, reach + tall)
        def _(index, ref=ref):
            clear_rows(ref, index)

    pl.semaphore_wait(barrier, count_dom + 1 + jnp.where(has_outer, 1, 0))

    def halo(source, target, index):
        right = remote(
            source.at[pl.ds(planes - ITERS, ITERS)], target.at[pl.ds(0, ITERS), body],
            halo_send.at[index], halo_recv.at[index], dom=dom + 1,
        )
        left = remote(
            source.at[pl.ds(0, ITERS)], target.at[pl.ds(ITERS + planes, ITERS), body],
            halo_send.at[index + 1], halo_recv.at[index + 1], dom=dom - 1,
        )
        return right, left

    halos = [halo(dielectric_ref, eps, 0), halo(start_ref, fields.at[0], 2)]
    depth = ITERS - 1

    def den(plane, right):
        spot = plane - (planes - depth) if right else plane
        here = density.at[depth + plane]
        there = density.at[spot] if right else density.at[depth + planes + spot]
        way = 0 if right else 1
        return remote(
            here, there, den_send.at[way, spot], den_recv.at[way, spot], dom=dom + 1 if right else dom - 1
        )

    def sides(pairs, start):
        @pl.when(has_right)
        def _():
            for right, left in pairs:
                if start:
                    right.start()
                else:
                    right.wait_send()
                    left.wait_recv()

        @pl.when(has_left)
        def _():
            for right, left in pairs:
                if start:
                    left.start()
                else:
                    left.wait_send()
                    right.wait_recv()

    sides(halos, True)

    def incoming(index, step):
        return remote(
            orbitals_ref.at[peer(step) * per + index],
            wave.at[index, pl.ds(reach + dom * planes, planes), body],
            in_send.at[index, step], in_recv.at[index, step], dom=peer(step),
        )

    bulk = [(index, step) for index in range(per) for step in range(1, count_dom)]

    def feed(start, stop):
        for index, step in bulk[start:stop]:
            incoming(index, step).start()

    feed(0, FEEDS[0])
    shares.wait()
    loads[0].wait()

    def to_inner(plane):
        return remote(acc.at[plane], part_in.at[plane], acc_send.at[plane], acc_recv.at[plane], band=inner)

    def cross(plane):
        return remote(acc.at[plane], other.at[plane], other_send.at[plane], other_recv.at[plane], band=inner)

    def back(plane, source):
        return remote(source.at[plane], side.at[plane], side_send.at[plane], side_recv.at[plane], band=outer)

    def relay(plane):
        return remote(other.at[plane], other.at[plane], relay_send.at[plane], other_recv.at[plane], band=outer)

    @pl.loop(0, planes)
    def _(plane):
        total = jnp.zeros((rows, lanes), jnp.float32)
        for index in range(norb):
            cells = orbs[index, plane]
            total = total + share[index] * cells * cells

        @pl.when(has_outer)
        def _():
            own[plane] = total

        @pl.when(jnp.logical_not(has_outer))
        def _():
            acc[plane] = total

            @pl.when(is_mid)
            def _():
                cross(plane).start()

            @pl.when(jnp.logical_not(is_mid))
            def _():
                to_inner(plane).start()

    @pl.when(has_outer)
    def _():
        @pl.loop(0, planes)
        def _(plane):
            to_inner(plane).wait_recv()
            acc[plane] = own[plane] + part_in[plane]

            @pl.when(is_mid)
            def _():
                cross(plane).start()
                back(plane, acc).start()

            @pl.when(jnp.logical_not(is_mid))
            def _():
                to_inner(plane).start()

    loads[1].wait()
    loads[2].wait()
    loads[3].wait()
    sides(halos, False)
    lane = lax.broadcasted_iota(jnp.int32, (rows, lanes), 1)
    row = lax.broadcasted_iota(jnp.int32, (rows, lanes), 0)
    zero = jnp.zeros((rows, lanes), jnp.float32)

    @pl.loop(1, extent - 1)
    def _(index):
        here = eps[index, body, :]
        ahead = jnp.where(lane < lanes - 1, pltpu.roll(here, lanes - 1, 1), zero)
        behind = jnp.where(lane > 0, pltpu.roll(here, 1, 1), zero)
        faces = (
            0.5 * (here + eps[index + 1, body, :]),
            0.5 * (here + eps[index - 1, body, :]),
            0.5 * (here + eps[index, wide + 1 : wide + 1 + rows, :]),
            0.5 * (here + eps[index, wide - 1 : wide - 1 + rows, :]),
            0.5 * (here + ahead),
            0.5 * (here + behind),
        )
        denominator = faces[0] + faces[1] + faces[2] + faces[3] + faces[4] + faces[5]
        cell = dom * planes + index - ITERS
        inside = jnp.logical_and(cell >= 0, cell < tall)
        factor = jnp.where(inside, 1.0 / jnp.where(inside, denominator, 1.0), zero)
        inverse[index] = 4.0 * factor
        for face in range(4):
            weights[face, index] = faces[face] * factor
        weights[4, index] = jnp.where(lane < lanes - 1, faces[4] * factor, zero)
        weights[5, index] = jnp.where(lane > 0, faces[5] * factor, zero)

    @pl.loop(0, planes)
    def _(plane):
        @pl.when(jnp.logical_not(is_mid))
        def _():
            back(plane, side).wait_recv()

            @pl.when(has_outer)
            def _():
                back(plane, side).start()

        cross(plane).wait_recv()

        @pl.when(has_outer)
        def _():
            relay(plane).start()

        @pl.when(is_mid)
        def _():
            density[depth + plane] = acc[plane] + other[plane]

        @pl.when(jnp.logical_not(is_mid))
        def _():
            density[depth + plane] = side[plane] + other[plane]

        @pl.when(jnp.logical_and(has_right, plane >= planes - depth))
        def _():
            den(plane, True).start()

        @pl.when(jnp.logical_and(has_left, plane < depth))
        def _():
            den(plane, False).start()

    feed(FEEDS[0], FEEDS[1])

    def sweep_at(turn, index):
        before, after = fields.at[turn], fields.at[turn + 1]
        here = before[index, body, :]
        total = density[index - 1] * inverse[index]
        total = total + (
            weights[0, index] * before[index + 1, body, :] + weights[1, index] * before[index - 1, body, :]
        )
        total = total + (
            weights[2, index] * before[index, wide + 1 : wide + 1 + rows, :]
            + weights[3, index] * before[index, wide - 1 : wide - 1 + rows, :]
        )
        total = total + (
            weights[4, index] * pltpu.roll(here, lanes - 1, 1) + weights[5, index] * pltpu.roll(here, 1, 1)
        )
        after[index, body, :] = total

    for turn in range(ITERS - 1):
        for index in range(ITERS + turn, ITERS + planes - turn):
            sweep_at(turn, index)

    @pl.when(has_left)
    def _():
        for spot in range(depth):
            den(planes - depth + spot, True).wait_recv()

    for turn in range(ITERS - 1):
        for index in range(1 + turn, 1 + turn + depth):
            sweep_at(turn, index)

    @pl.when(has_right)
    def _():
        for spot in range(depth):
            den(spot, False).wait_recv()

    for turn in range(ITERS - 1):
        for index in range(extent - 1 - turn - depth, extent - 1 - turn):
            sweep_at(turn, index)

    def potential_at(plane):
        sweep_at(ITERS - 1, ITERS + plane)
        cells = density[depth + plane] + core[plane]
        root = jnp.exp(jnp.log(cells) * (1.0 / 3.0))
        root = root - (root - cells / (root * root)) * (1.0 / 3.0)
        pot = fields[ITERS, ITERS + plane, body, :] + slater * root
        pot_own[plane] = pot
        strength[dom * planes + plane] = (pot - (center_value + 1.5 * coeff_zero)) * (2.0 / half_value)

    mine = pl.ds(dom * planes, planes)
    chips = count_dom // 2
    half = planes // 2
    odd = lax.rem(band, 2)
    mate = band + 1 - 2 * odd

    def piece(step, which):
        return pl.ds(lax.rem(dom + count_dom - 2 * step, count_dom) * planes + which * half, half)

    def spread(step):
        if step == 0:
            return remote(
                strength.at[mine], strength.at[mine], pot_send.at[0], pot_recv.at[0], dom=partner
            )
        here = strength.at[piece(0, odd)]
        return remote(here, here, pot_send.at[step], pot_recv.at[step], dom=peer(2 * step))

    def swap(step):
        here = strength.at[piece(step, odd)]
        return remote(here, here, swap_send.at[step], swap_recv.at[step], band=mate)

    def hand(step, late):
        here = strength.at[piece(step, 1 - odd if late else odd)]
        return remote(here, here, pass_send.at[step, late], pass_recv.at[step, late], dom=partner)

    steps = range(chips - 1, 0, -1)

    @pl.loop(0, half)
    def _(plane):
        potential_at(odd * half + plane)

    for step in steps:
        spread(step).start()
    feed(FEEDS[1], FEEDS[2])

    @pl.loop(0, half)
    def _(plane):
        potential_at((1 - odd) * half + plane)

    spread(0).start()
    feed(FEEDS[2], len(bulk))
    keep = pltpu.make_async_copy(pot_own, potential_ref, end_sem.at[0])
    keep.start()
    for step in steps:
        spread(step).wait_recv()
        swap(step).start()
        hand(step, 0).start()
    for step in steps:
        swap(step).wait_recv()
        hand(step, 1).start()
    spread(0).wait_recv()

    gap = jnp.abs(
        lax.broadcasted_iota(jnp.int32, (2 * lanes, lanes), 0) % lanes
        - lax.broadcasted_iota(jnp.int32, (2 * lanes, lanes), 1)
    )
    weight = jnp.where(gap == 1, 135.0, jnp.where(gap == 2, -13.5, jnp.where(gap == 3, 1.0, 0.0)))
    stripes[...] = weight.astype(jnp.bfloat16)
    scale = -coeff_three / half_value

    units = tall // reach
    parts = planes // reach
    span = 2 * parts
    origin = (dom // 2) * span

    def double_h(level, ref, base, put):
        cells = ref[pl.ds(reach + base, reach), body, :].reshape(reach * rows, lanes)
        high = cells.astype(jnp.bfloat16)
        rest = cells - high.astype(jnp.float32)
        mid = rest.astype(jnp.bfloat16)
        low = (rest - mid.astype(jnp.float32)).astype(jnp.bfloat16)
        lines = jnp.dot(
            jnp.concatenate([high, mid], axis=1), stripes[...], preferred_element_type=jnp.float32
        ) + jnp.dot(low, stripes[:lanes], preferred_element_type=jnp.float32)
        sums[level] = lines.reshape(reach, rows, lanes)
        for local_plane in range(reach):
            at = base + local_plane
            here = ref[reach + at, body, :]

            def around(dist):
                along = ref[reach + at + dist, body, :] + ref[reach + at - dist, body, :]
                return along + (
                    ref[reach + at, wide + dist : wide + dist + rows, :]
                    + ref[reach + at, wide - dist : wide - dist + rows, :]
                )

            total = sums[level, local_plane] + around(3)
            total = total + 135.0 * around(1) - 13.5 * around(2)
            put(at, strength[at] * here + scale * total)

    def leave(index, unit):
        block = unit // parts
        step = lax.rem(block - dom + count_dom, count_dom)
        part = lax.rem(unit, parts)
        here = result.at[index, pl.ds(unit * reach, reach)]
        there = filtered_ref.at[dom * per + index, pl.ds(part * reach, reach)]
        away = remote(here, there, out_send.at[index, step, part], out_recv.at[index, step, part], dom=block)
        return step, away, pltpu.make_async_copy(here, there, end_sem.at[1 + index * parts + part])

    def advance(level, tick):
        spot = tick - 2 * level

        @pl.when(jnp.logical_and(spot >= 0, spot < per * units))
        def _():
            index = spot // units
            unit = lax.rem(origin + spot + level, units)
            even, odds = wave.at[index], wave_next.at[index]

            if level == 0:
                def put(at, value):
                    odds[reach + at, body, :] = 0.5 * value
            elif level < DEGREE - 1:
                onto = even if level % 2 else odds

                def put(at, value):
                    onto[reach + at, body, :] = value - onto[reach + at, body, :]
            else:
                def put(at, value):
                    result[index, at] = value - even[reach + at, body, :]

            double_h(level, odds if level % 2 else even, unit * reach, put)
            if level == DEGREE - 1:
                step, away, home = leave(index, unit)

                @pl.when(step > 0)
                def _():
                    away.start()

                @pl.when(step == 0)
                def _():
                    home.start()

    @pl.loop(0, per * units + 2 * (DEGREE - 1))
    def _(tick):
        @pl.when(jnp.logical_and(lax.rem(tick, units) == 0, tick < per * units))
        def _():
            index = tick // units
            pltpu.make_async_copy(
                orbitals_ref.at[dom * per + index],
                wave.at[index, pl.ds(reach + dom * planes, planes), body],
                load_sem.at[4 + index],
            ).wait()
            for step in range(1, count_dom):
                incoming(index, step).wait_recv()

        for turn in range(1, chips):
            @pl.when(tick == turn * span)
            def _(step=chips - turn):
                hand(step, 0).wait_recv()
                hand(step, 1).wait_recv()

        for level in range(DEGREE):
            advance(level, tick)

    for step in range(chips):
        spread(step).wait_send()
    for step in range(1, chips):
        swap(step).wait_send()
        hand(step, 0).wait_send()
        hand(step, 1).wait_send()
    for index in range(per):
        for step in range(1, count_dom):
            incoming(index, step).wait_send()

    @pl.loop(0, planes)
    def _(plane):
        @pl.when(is_mid)
        def _():
            cross(plane).wait_send()

        @pl.when(jnp.logical_not(is_mid))
        def _():
            to_inner(plane).wait_send()

        @pl.when(has_outer)
        def _():
            back(plane, acc).wait_send()
            relay(plane).wait_send()

        @pl.when(jnp.logical_and(has_right, plane >= planes - depth))
        def _():
            den(plane, True).wait_send()

        @pl.when(jnp.logical_and(has_left, plane < depth))
        def _():
            den(plane, False).wait_send()

    keep.wait()
    for index in range(per):
        for part in range(parts):
            leave(index, dom * parts + part)[2].wait()
            for step in range(1, count_dom):
                leave(index, peer(step) * parts + part)[1].wait()


def deliver(direct, held_pot, held_filtered, potential_ref, filtered_ref, buf, pot_buf, in_sem, out_sem):
    norb = held_filtered.shape[0]
    if direct:
        puts = [pltpu.make_async_copy(held_pot, potential_ref, out_sem.at[norb])]
        puts += [pltpu.make_async_copy(held_filtered.at[i], filtered_ref.at[i], out_sem.at[i]) for i in range(norb)]
        for put in puts:
            put.start()
    else:
        gets = [pltpu.make_async_copy(held_pot, pot_buf, in_sem.at[norb])]
        gets += [pltpu.make_async_copy(held_filtered.at[i], buf.at[i], in_sem.at[i]) for i in range(norb)]
        puts = [pltpu.make_async_copy(pot_buf, potential_ref, out_sem.at[norb])]
        puts += [pltpu.make_async_copy(buf.at[i], filtered_ref.at[i], out_sem.at[i]) for i in range(norb)]
        for get in gets:
            get.start()
        for get, put in zip(gets, puts):
            get.wait()
            put.start()
    for put in puts:
        put.wait()


def fast(count_band, count_dom, orbitals, occupation, dielectric, core_density, start_field):
    norb, planes, rows, lanes = orbitals.shape
    per = norb // count_dom
    tall = count_dom * planes
    extent = planes + 2 * ITERS
    high = rows + 16
    chips = count_dom // 2

    def vmem(*shape):
        return pltpu.VMEM(shape, jnp.float32)

    def dma(*shape):
        return pltpu.SemaphoreType.DMA(shape)

    parts = planes // 3
    scratch = [
        vmem(norb, planes, rows, lanes),
        pltpu.SMEM((norb,), jnp.float32),
        vmem(planes, rows, lanes),
        vmem(planes, rows, lanes),
        vmem(planes, rows, lanes),
        vmem(planes, rows, lanes),
        vmem(planes, rows, lanes),
        vmem(planes + 2 * (ITERS - 1), rows, lanes),
        vmem(extent, high, lanes),
        vmem(ITERS + 1, extent, high, lanes),
        vmem(6, extent, rows, lanes),
        vmem(extent, rows, lanes),
        vmem(planes, rows, lanes),
        vmem(planes, rows, lanes),
        vmem(tall, rows, lanes),
        vmem(per, tall + 6, high, lanes),
        vmem(per, tall + 6, high, lanes),
        vmem(per, tall, rows, lanes),
        pltpu.VMEM((2 * lanes, lanes), jnp.bfloat16),
        vmem(DEGREE, 3, rows, lanes),
        dma(4 + per),
        dma(1),
        dma(4), dma(4),
        dma(per, count_dom), dma(per, count_dom),
        dma(planes), dma(planes),
        dma(planes), dma(planes),
        dma(planes), dma(planes),
        dma(planes),
        dma(2, ITERS - 1), dma(2, ITERS - 1),
        dma(chips), dma(chips),
        dma(chips), dma(chips),
        dma(chips, 2), dma(chips, 2),
        dma(per, count_dom, parts), dma(per, count_dom, parts),
        dma(1 + per * parts),
    ]

    def kernel(*refs):
        exchange(count_band, count_dom, refs[:5], refs[5], refs[6], refs[7:])

    hbm = pl.BlockSpec(memory_space=pl.ANY)

    def pin(array):
        return pltpu.with_memory_space_constraint(array, pltpu.HBM)

    held = pl.pallas_call(
        kernel,
        out_shape=(
            jax.ShapeDtypeStruct((planes, rows, lanes), jnp.float32),
            jax.ShapeDtypeStruct(orbitals.shape, jnp.float32),
        ),
        in_specs=[hbm] * 5,
        out_specs=(hbm, hbm),
        scratch_shapes=scratch,
        compiler_params=pltpu.CompilerParams(
            collective_id=0, has_side_effects=True, vmem_limit_bytes=40 * 1024 * 1024
        ),
        name="filter_whole",
    )(pin(orbitals), pin(occupation), pin(dielectric), pin(core_density), pin(start_field))
    hold = (planes, rows, lanes) if not True else (8, 8, 128)
    return pl.pallas_call(
        functools.partial(deliver, True),
        out_shape=(
            jax.ShapeDtypeStruct((planes, rows, lanes), jnp.float32),
            jax.ShapeDtypeStruct(orbitals.shape, jnp.float32),
        ),
        in_specs=[hbm, hbm],
        out_specs=(hbm, hbm),
        scratch_shapes=[vmem(norb, *hold), vmem(*hold), dma(norb + 1), dma(norb + 1)],
        compiler_params=pltpu.CompilerParams(vmem_limit_bytes=16 * 1024 * 1024),
        name="deliver",
    )(*held)


def program(count_band, count_dom, *arrays):
    norb, planes, rows, lanes = arrays[0].shape
    suits = (
        norb % count_dom == 0
        and count_dom % 2 == 0
        and count_dom > 2
        and count_band % 2 == 0
        and planes >= ITERS
        and planes % 6 == 0
        and rows % 8 == 0
        and lanes == 128
    )
    if suits:
        return fast(count_band, count_dom, *arrays)
    return local(*arrays)


def solution(mesh):
    return jax.shard_map(
        functools.partial(program, mesh.shape["band"], mesh.shape["dom"]),
        mesh=mesh,
        in_specs=(
            P("band", "dom", None, None),
            P("band"),
            P("dom", None, None),
            P("dom", None, None),
            P("dom", None, None),
        ),
        out_specs=(P("dom", None, None), P("band", "dom", None, None)),
        check_vma=False,
    )
```

```python
import functools

import jax
import jax.numpy as jnp
from jax import lax
from jax.experimental import pallas as pl
from jax.experimental.pallas import tpu as pltpu
from jax.sharding import PartitionSpec as P

ITERS = 4
DEGREE = 4


coeff_one = 1.5
coeff_two = -0.15
coeff_three = 1.0 / 90.0
coeff_zero = -49.0 / 18.0
center_value = 5.25
half_value = 4.75
slater = -0.9847450218426964


def padded_2(cells, sides, width):
    for axis, dim in sides:
        count = lax.axis_size(axis)
        ends = count - 1
        head = lax.slice_in_dim(cells, 0, width, axis=dim)
        tail = lax.slice_in_dim(cells, cells.shape[dim] - width, cells.shape[dim], axis=dim)
        cells = jnp.concatenate(
            [
                lax.ppermute(tail, axis, [(i, (i + 1) % count) for i in range(ends)]),
                cells,
                lax.ppermute(head, axis, [((i + 1) % count, i) for i in range(ends)]),
            ],
            axis=dim,
        )
    return cells


def laplace(padded):
    size_x = padded.shape[-3] - 6
    size_y = padded.shape[-2] - 6
    size_z = padded.shape[-1] - 6
    core = padded[..., 3 : 3 + size_x, 3 : 3 + size_y, 3 : 3 + size_z]
    total = 3.0 * coeff_zero * core
    for dist, weight in ((1, coeff_one), (2, coeff_two), (3, coeff_three)):
        along = padded[..., 3 + dist : 3 + dist + size_x, 3 : 3 + size_y, 3 : 3 + size_z]
        along = along + padded[..., 3 - dist : 3 - dist + size_x, 3 : 3 + size_y, 3 : 3 + size_z]
        along = along + padded[..., 3 : 3 + size_x, 3 + dist : 3 + dist + size_y, 3 : 3 + size_z]
        along = along + padded[..., 3 : 3 + size_x, 3 - dist : 3 - dist + size_y, 3 : 3 + size_z]
        along = along + padded[..., 3 : 3 + size_x, 3 : 3 + size_y, 3 + dist : 3 + dist + size_z]
        along = along + padded[..., 3 : 3 + size_x, 3 : 3 + size_y, 3 - dist : 3 - dist + size_z]
        total = total + weight * along
    return total


def face_weights(permit, padded):
    weights = (
        0.5 * (permit + padded[2:, 1:-1, 1:-1]),
        0.5 * (permit + padded[:-2, 1:-1, 1:-1]),
        0.5 * (permit + padded[1:-1, 2:, 1:-1]),
        0.5 * (permit + padded[1:-1, :-2, 1:-1]),
        0.5 * (permit + padded[1:-1, 1:-1, 2:]),
        0.5 * (permit + padded[1:-1, 1:-1, :-2]),
    )
    denominator = weights[0] + weights[1] + weights[2] + weights[3] + weights[4] + weights[5]
    return (weights, denominator)


def sweep(padded, weights, denominator, source):
    numerator = weights[0] * padded[2:, 1:-1, 1:-1] + weights[1] * padded[:-2, 1:-1, 1:-1]
    numerator = (
        numerator + weights[2] * padded[1:-1, 2:, 1:-1] + weights[3] * padded[1:-1, :-2, 1:-1]
    )
    numerator = (
        numerator + weights[4] * padded[1:-1, 1:-1, 2:] + weights[5] * padded[1:-1, 1:-1, :-2]
    )
    return (numerator + source) / denominator


def copies_rim(block):
    padded = padded_2(block, (("dom", 0),), 1)
    return jnp.pad(padded, ((0, 0), (1, 1), (1, 1)))


def apply_extended(padded_x, pot):
    padded = jnp.pad(padded_x, ((0, 0), (0, 0), (3, 3), (3, 3)))
    inner = padded_x[:, 3:-3]
    return -0.5 * laplace(padded) + pot[None] * inner


def local(orbitals, occupation, dielectric, core_density, start_field):
    partial_density = jnp.sum(occupation[:, None, None, None] * orbitals * orbitals, axis=0)
    density = lax.psum(partial_density, "band")
    permit_pad = padded_2(dielectric, (("dom", 0),), 1)
    permit_pad = jnp.pad(permit_pad, ((0, 0), (1, 1), (1, 1)))
    weights, denominator = face_weights(dielectric, permit_pad)
    source = 4.0 * density
    field = start_field
    for turn_index in range(ITERS):
        field = sweep(copies_rim(field), weights, denominator, source)
    potential = field + slater * jnp.cbrt(density + core_density)

    def hamil(block):
        padded = padded_2(block, (("dom", 1),), 3)
        return apply_extended(padded, potential)

    before = orbitals
    current = (hamil(orbitals) - center_value * orbitals) / half_value
    for turn_index in range(DEGREE - 1):
        nextone = 2.0 * (hamil(current) - center_value * current) / half_value - before
        before = current
        current = nextone
    return (potential, current)


MESH = pl.DeviceIdType.MESH
FEEDS = (5, 7, 14)
SWAP_AHEAD = 2


def exchange(count_band, count_dom, refs_in, potential_ref, filtered_ref, scratch):
    orbitals_ref, occupation_ref, dielectric_ref, core_ref, start_ref = refs_in
    (
        orbs, share, own, part_in, side, other, acc, density, eps, fields, weights, inverse,
        core, pot_own, strength, wave, later_one, later_two, later_three, result, stripes, sums,
        load_sem, share_sem, halo_send, halo_recv, in_send, in_recv, acc_send, acc_recv,
        side_send, side_recv, other_send, other_recv, relay_send,
        den_send, den_recv, pot_send, pot_recv, swap_send, swap_recv, mate_send, mate_recv, pass_send, pass_recv, out_send, out_recv, end_sem,
    ) = scratch
    later = (later_one, later_two, later_three)
    norb, planes, rows, lanes = orbitals_ref.shape
    per = norb // count_dom
    wide = 8
    reach = 3
    band = lax.axis_index("band")
    dom = lax.axis_index("dom")
    middle = count_band // 2
    in_left = band < middle
    toward = jnp.where(in_left, 1, -1)
    inner = band + toward
    outer = band - toward
    has_outer = jnp.logical_and(band > 0, band < count_band - 1)
    is_mid = jnp.logical_or(band == middle - 1, band == middle)
    has_left = dom > 0
    has_right = dom < count_dom - 1
    partner = dom + 1 - 2 * lax.rem(dom, 2)
    body = pl.ds(wide, rows)
    half = planes // 2
    chips = count_dom // 2
    odd = lax.rem(band, 2)
    mate = band + 1 - 2 * odd
    shift = odd * half

    def peer(step):
        return lax.rem(dom + step, count_dom)

    def remote(src, dst, send, recv, **where):
        return pltpu.make_async_remote_copy(
            src_ref=src, dst_ref=dst, send_sem=send, recv_sem=recv, device_id=where, device_id_type=MESH
        )

    loads = [
        pltpu.make_async_copy(orbitals_ref, orbs, load_sem.at[0]),
        pltpu.make_async_copy(dielectric_ref, eps.at[pl.ds(ITERS, planes), body], load_sem.at[1]),
        pltpu.make_async_copy(start_ref, fields.at[0, pl.ds(ITERS, planes), body], load_sem.at[2]),
        pltpu.make_async_copy(core_ref, core, load_sem.at[3]),
    ]
    for index in range(per):
        loads.append(
            pltpu.make_async_copy(
                orbitals_ref.at[dom * per + index],
                wave.at[index, pl.ds(reach + dom * planes, planes), body],
                load_sem.at[4 + index],
            )
        )
    shares = pltpu.make_async_copy(occupation_ref, share, share_sem.at[0])
    shares.start()
    for copy in loads:
        copy.start()

    barrier = pltpu.get_barrier_semaphore()
    for step in range(1, count_dom):
        pl.semaphore_signal(barrier, inc=1, device_id={"dom": peer(step)}, device_id_type=MESH)
    pl.semaphore_signal(barrier, inc=1, device_id={"band": inner}, device_id_type=MESH)
    pl.semaphore_signal(barrier, inc=1, device_id={"band": band + 1 - 2 * lax.rem(band, 2)}, device_id_type=MESH)

    @pl.when(has_outer)
    def _():
        pl.semaphore_signal(barrier, inc=1, device_id={"band": outer}, device_id_type=MESH)

    def clear_rows(ref, index):
        ref[index, :wide, :] = jnp.zeros((wide, lanes), jnp.float32)
        ref[index, wide + rows :, :] = jnp.zeros((wide, lanes), jnp.float32)

    def clear_plane(ref, index):
        ref[index] = jnp.zeros(ref.shape[1:], jnp.float32)

    extent = planes + 2 * ITERS

    @pl.loop(0, extent)
    def _(index):
        clear_rows(eps, index)
        for turn in range(ITERS):
            clear_rows(fields.at[turn], index)

    @pl.when(jnp.logical_not(has_left))
    def _():
        for index in range(ITERS):
            eps[index, body, :] = jnp.zeros((rows, lanes), jnp.float32)
            fields[0, index, body, :] = jnp.zeros((rows, lanes), jnp.float32)
        for index in range(ITERS - 1):
            density[index] = jnp.zeros((rows, lanes), jnp.float32)

    @pl.when(jnp.logical_not(has_right))
    def _():
        for index in range(ITERS):
            eps[ITERS + planes + index, body, :] = jnp.zeros((rows, lanes), jnp.float32)
            fields[0, ITERS + planes + index, body, :] = jnp.zeros((rows, lanes), jnp.float32)
        for index in range(ITERS - 1):
            density[ITERS - 1 + planes + index] = jnp.zeros((rows, lanes), jnp.float32)

    tall = count_dom * planes
    for ref in [stack.at[index] for stack in (wave, *later) for index in range(per)]:
        for index in range(reach):
            clear_plane(ref, index)
            clear_plane(ref, reach + tall + index)

        @pl.loop(reach, reach + tall)
        def _(index, ref=ref):
            clear_rows(ref, index)

    gap = jnp.abs(
        lax.broadcasted_iota(jnp.int32, (2 * lanes, lanes), 0) % lanes
        - lax.broadcasted_iota(jnp.int32, (2 * lanes, lanes), 1)
    )
    weight = jnp.where(gap == 1, 135.0, jnp.where(gap == 2, -13.5, jnp.where(gap == 3, 1.0, 0.0)))
    stripes[...] = weight.astype(jnp.bfloat16)
    scale = -coeff_three / half_value

    pl.semaphore_wait(barrier, count_dom + 1 + jnp.where(has_outer, 1, 0))

    reserve = max(ITERS - half, 1)

    def halo(source, target, index, deep_left):
        from_left, from_right = (ITERS, reserve) if deep_left else (reserve, ITERS)
        right = remote(
            source.at[pl.ds(planes - from_left, from_left)], target.at[pl.ds(ITERS - from_left, from_left), body],
            halo_send.at[index], halo_recv.at[index], dom=dom + 1,
        )
        left = remote(
            source.at[pl.ds(0, from_right)], target.at[pl.ds(ITERS + planes, from_right), body],
            halo_send.at[index + 1], halo_recv.at[index + 1], dom=dom - 1,
        )
        return right, left

    depth = ITERS - 1

    def den(plane, right):
        spot = plane - (planes - depth) if right else plane
        here = density.at[depth + plane]
        there = density.at[spot] if right else density.at[depth + planes + spot]
        way = 0 if right else 1
        return remote(
            here, there, den_send.at[way, spot], den_recv.at[way, spot], dom=dom + 1 if right else dom - 1
        )

    def sides(start):
        for parity in range(2):
            for here, mine, theirs in ((has_right, 0, 1), (has_left, 1, 0)):
                @pl.when(jnp.logical_and(odd == parity, here))
                def _(parity=parity, mine=mine, theirs=theirs):
                    for source, target, index in ((dielectric_ref, eps, 0), (start_ref, fields.at[0], 2)):
                        pair = halo(source, target, index, parity == 0)
                        if start:
                            pair[mine].start()
                        else:
                            pair[mine].wait_send()
                            pair[theirs].wait_recv()

    sides(True)

    def incoming(index, step):
        return remote(
            orbitals_ref.at[peer(step) * per + index],
            wave.at[index, pl.ds(reach + dom * planes, planes), body],
            in_send.at[index, step], in_recv.at[index, step], dom=peer(step),
        )

    bulk = [(index, step) for index in range(per) for step in range(1, count_dom)]

    def feed(start, stop):
        for index, step in bulk[start:stop]:
            incoming(index, step).start()

    held = lax.rem(dom + band, 2) == 1
    feed(0, FEEDS[0])

    @pl.when(jnp.logical_not(held))
    def _():
        feed(FEEDS[0], FEEDS[1])

    shares.wait()
    loads[0].wait()

    def to_inner(plane):
        return remote(acc.at[plane], part_in.at[plane], acc_send.at[plane], acc_recv.at[plane], band=inner)

    def cross(plane):
        return remote(acc.at[plane], other.at[plane], other_send.at[plane], other_recv.at[plane], band=inner)

    def back(plane, source):
        return remote(source.at[plane], side.at[plane], side_send.at[plane], side_recv.at[plane], band=outer)

    def relay(plane):
        return remote(other.at[plane], other.at[plane], relay_send.at[plane], other_recv.at[plane], band=outer)

    @pl.loop(0, planes)
    def _(plane):
        total = jnp.zeros((rows, lanes), jnp.float32)
        for index in range(norb):
            cells = orbs[index, plane]
            total = total + share[index] * cells * cells

        @pl.when(has_outer)
        def _():
            own[plane] = total

        @pl.when(jnp.logical_not(has_outer))
        def _():
            acc[plane] = total

            @pl.when(is_mid)
            def _():
                cross(plane).start()

            @pl.when(jnp.logical_not(is_mid))
            def _():
                to_inner(plane).start()

    @pl.when(has_outer)
    def _():
        @pl.loop(0, planes)
        def _(plane):
            to_inner(plane).wait_recv()
            acc[plane] = own[plane] + part_in[plane]

            @pl.when(is_mid)
            def _():
                cross(plane).start()
                back(plane, acc).start()

            @pl.when(jnp.logical_not(is_mid))
            def _():
                to_inner(plane).start()

    def settle():
        loads[1].wait()
        loads[2].wait()
        loads[3].wait()
        sides(False)
        lane = lax.broadcasted_iota(jnp.int32, (rows, lanes), 1)
        row = lax.broadcasted_iota(jnp.int32, (rows, lanes), 0)
        zero = jnp.zeros((rows, lanes), jnp.float32)

        @pl.loop(0, half + 2 * depth)
        def _(spot):
            index = 1 + shift + spot
            here = eps[index, body, :]
            ahead = jnp.where(lane < lanes - 1, pltpu.roll(here, lanes - 1, 1), zero)
            behind = jnp.where(lane > 0, pltpu.roll(here, 1, 1), zero)
            faces = (
                0.5 * (here + eps[index + 1, body, :]),
                0.5 * (here + eps[index - 1, body, :]),
                0.5 * (here + eps[index, wide + 1 : wide + 1 + rows, :]),
                0.5 * (here + eps[index, wide - 1 : wide - 1 + rows, :]),
                0.5 * (here + ahead),
                0.5 * (here + behind),
            )
            denominator = faces[0] + faces[1] + faces[2] + faces[3] + faces[4] + faces[5]
            cell = dom * planes + index - ITERS
            inside = jnp.logical_and(cell >= 0, cell < tall)
            factor = jnp.where(inside, 1.0 / jnp.where(inside, denominator, 1.0), zero)
            inverse[index] = 4.0 * factor
            for face in range(4):
                weights[face, index] = faces[face] * factor
            weights[4, index] = jnp.where(lane < lanes - 1, faces[4] * factor, zero)
            weights[5, index] = jnp.where(lane > 0, faces[5] * factor, zero)

    pl.when(jnp.logical_not(is_mid))(settle)

    @pl.loop(0, planes)
    def _(plane):
        @pl.when(jnp.logical_not(is_mid))
        def _():
            back(plane, side).wait_recv()

            @pl.when(has_outer)
            def _():
                back(plane, side).start()

        cross(plane).wait_recv()

        @pl.when(has_outer)
        def _():
            relay(plane).start()

        @pl.when(is_mid)
        def _():
            density[depth + plane] = acc[plane] + other[plane]

        @pl.when(jnp.logical_not(is_mid))
        def _():
            density[depth + plane] = side[plane] + other[plane]

        @pl.when(jnp.logical_and(jnp.logical_and(odd == 0, has_right), plane >= planes - depth))
        def _():
            den(plane, True).start()

        @pl.when(jnp.logical_and(jnp.logical_and(odd == 1, has_left), plane < depth))
        def _():
            den(plane, False).start()

    pl.when(is_mid)(settle)

    @pl.when(held)
    def _():
        feed(FEEDS[0], FEEDS[1])

    def sweep_at(turn, index):
        before, after = fields.at[turn], fields.at[turn + 1]
        here = before[index, body, :]
        total = density[index - 1] * inverse[index]
        total = total + (
            weights[0, index] * before[index + 1, body, :] + weights[1, index] * before[index - 1, body, :]
        )
        total = total + (
            weights[2, index] * before[index, wide + 1 : wide + 1 + rows, :]
            + weights[3, index] * before[index, wide - 1 : wide - 1 + rows, :]
        )
        total = total + (
            weights[4, index] * pltpu.roll(here, lanes - 1, 1) + weights[5, index] * pltpu.roll(here, 1, 1)
        )
        after[index, body, :] = total

    for turn in range(ITERS - 1):
        first = turn + jnp.where(odd == 0, ITERS, 1 + half)
        for spot in range(half + depth - 2 * turn):
            sweep_at(turn, first + spot)

    @pl.when(jnp.logical_and(odd == 0, has_left))
    def _():
        for spot in range(depth):
            den(planes - depth + spot, True).wait_recv()

    @pl.when(jnp.logical_and(odd == 1, has_right))
    def _():
        for spot in range(depth):
            den(spot, False).wait_recv()

    for turn in range(ITERS - 1):
        first = jnp.where(odd == 0, 1 + turn, ITERS + planes - turn)
        for spot in range(depth):
            sweep_at(turn, first + spot)

    def potential_at(plane):
        sweep_at(ITERS - 1, ITERS + plane)
        cells = density[depth + plane] + core[plane]
        root = jnp.exp(jnp.log(cells) * (1.0 / 3.0))
        root = root - (root - cells / (root * root)) * (1.0 / 3.0)
        pot = fields[ITERS, ITERS + plane, body, :] + slater * root
        pot_own[plane] = pot
        strength[dom * planes + plane] = (pot - (center_value + 1.5 * coeff_zero)) * (2.0 / half_value)

    mine = pl.ds(dom * planes, planes)

    def piece(step, which):
        return pl.ds(lax.rem(dom + count_dom - 2 * step, count_dom) * planes + which * half, half)

    near = jnp.where(lax.rem(dom // 2, 2) == 0, chips - 1, 1)
    order = [near] + [2 * pair for pair in range(1, chips // 2)]
    order += [lax.rem(near + 2 * pair, chips) for pair in range(1, chips // 2)]

    def spread(step):
        here = strength.at[piece(0, odd)]
        return remote(here, here, pot_send.at[step], pot_recv.at[step], dom=peer(2 * step))

    def share_pot():
        here = pot_own.at[pl.ds(shift, half)]
        return remote(here, here, mate_send.at[0], mate_recv.at[0], band=mate)

    def swap(step):
        here = strength.at[piece(step, odd)]
        return remote(here, here, swap_send.at[step], swap_recv.at[step], band=mate)

    def hand(step, late):
        here = strength.at[piece(step, 1 - odd if late else odd)]
        return remote(here, here, pass_send.at[step, late], pass_recv.at[step, late], dom=partner)

    @pl.loop(0, half)
    def _(spot):
        potential_at(shift + spot)

    for step in order:
        spread(chips - step).start()
    swap(0).start()
    hand(0, 0).start()
    share_pot().start()
    feed(FEEDS[1], FEEDS[2])

    def pass_on(step):
        spread(step).wait_recv()
        swap(step).start()
        hand(step, 0).start()

    for step in order[: chips // 2]:
        pass_on(step)
    swap(0).wait_recv()
    hand(0, 1).start()
    feed(FEEDS[2], len(bulk))
    for step in order[chips // 2 :]:
        pass_on(step)

    units = tall // reach
    parts = planes // reach
    span = 2 * parts
    origin = (dom // 2) * span

    levels = (wave, *later)

    def place(level, tick):
        spot = jnp.maximum(tick - 3 * level, 0)
        return jnp.minimum(spot // units, per - 1), lax.rem(origin + level + spot, units)

    def advance(tick):
        places = [place(level, tick) for level in range(DEGREE)]
        sources = [levels[level].at[places[level][0]] for level in range(DEGREE)]
        cells = jnp.concatenate(
            [
                sources[level][pl.ds(reach + places[level][1] * reach, reach), body, :].reshape(reach * rows, lanes)
                for level in range(DEGREE)
            ],
            axis=0,
        )
        high = cells.astype(jnp.bfloat16)
        rest = cells - high.astype(jnp.float32)
        mid = rest.astype(jnp.bfloat16)
        low = (rest - mid.astype(jnp.float32)).astype(jnp.bfloat16)
        lines = jnp.dot(
            jnp.concatenate([high, mid], axis=1), stripes[...], preferred_element_type=jnp.float32
        ) + jnp.dot(low, stripes[:lanes], preferred_element_type=jnp.float32)
        sums[...] = lines.reshape(DEGREE, reach, rows, lanes)
        for level in reversed(range(DEGREE)):
            index, unit = places[level]
            ref = sources[level]
            for local_plane in range(reach):
                at = unit * reach + local_plane
                here = ref[reach + at, body, :]

                def around(dist):
                    along = ref[reach + at + dist, body, :] + ref[reach + at - dist, body, :]
                    return along + (
                        ref[reach + at, wide + dist : wide + dist + rows, :]
                        + ref[reach + at, wide - dist : wide - dist + rows, :]
                    )

                total = sums[level, local_plane] + around(3)
                total = total + 135.0 * around(1) - 13.5 * around(2)
                value = strength[at] * here + scale * total
                if level == 0:
                    value = 0.5 * value
                else:
                    value = value - levels[level - 1][index, reach + at, body, :]
                if level < DEGREE - 1:
                    levels[level + 1][index, reach + at, body, :] = value
                else:
                    result[index, at] = value

    def leave(index, unit):
        block = unit // parts
        step = lax.rem(block - dom + count_dom, count_dom)
        part = lax.rem(unit, parts)
        here = result.at[index, pl.ds(unit * reach, reach)]
        there = filtered_ref.at[dom * per + index, pl.ds(part * reach, reach)]
        away = remote(here, there, out_send.at[index, step, part], out_recv.at[index, step, part], dom=block)
        return step, away, pltpu.make_async_copy(here, there, end_sem.at[1 + index * parts + part])

    hand(0, 0).wait_recv()
    hand(0, 1).wait_recv()

    @pl.loop(0, per * units + 3 * (DEGREE - 1))
    def _(tick):
        @pl.when(jnp.logical_and(lax.rem(tick, units) == 0, tick < per * units))
        def _():
            index = tick // units
            pltpu.make_async_copy(
                orbitals_ref.at[dom * per + index],
                wave.at[index, pl.ds(reach + dom * planes, planes), body],
                load_sem.at[4 + index],
            ).wait()
            for step in range(1, count_dom):
                incoming(index, step).wait_recv()

        for ahead in range(1, chips):
            @pl.when(tick == ahead * span - SWAP_AHEAD)
            def _(step=chips - ahead):
                swap(step).wait_recv()
                hand(step, 1).start()

            @pl.when(tick == ahead * span)
            def _(step=chips - ahead):
                hand(step, 0).wait_recv()
                hand(step, 1).wait_recv()

        advance(tick)

        @pl.when(tick >= 3 * (DEGREE - 1))
        def _():
            step, away, home = leave(*place(DEGREE - 1, tick))

            @pl.when(step > 0)
            def _():
                away.start()

            @pl.when(step == 0)
            def _():
                home.start()

    share_pot().wait()
    keep = pltpu.make_async_copy(pot_own, potential_ref, end_sem.at[0])
    keep.start()
    for step in range(1, chips):
        spread(step).wait_send()
    for step in range(chips):
        swap(step).wait_send()
        hand(step, 0).wait_send()
        hand(step, 1).wait_send()
    for index in range(per):
        for step in range(1, count_dom):
            incoming(index, step).wait_send()

    @pl.loop(0, planes)
    def _(plane):
        @pl.when(is_mid)
        def _():
            cross(plane).wait_send()

        @pl.when(jnp.logical_not(is_mid))
        def _():
            to_inner(plane).wait_send()

        @pl.when(has_outer)
        def _():
            back(plane, acc).wait_send()
            relay(plane).wait_send()

        @pl.when(jnp.logical_and(jnp.logical_and(odd == 0, has_right), plane >= planes - depth))
        def _():
            den(plane, True).wait_send()

        @pl.when(jnp.logical_and(jnp.logical_and(odd == 1, has_left), plane < depth))
        def _():
            den(plane, False).wait_send()

    keep.wait()
    for index in range(per):
        for part in range(parts):
            leave(index, dom * parts + part)[2].wait()
            for step in range(1, count_dom):
                leave(index, peer(step) * parts + part)[1].wait()


def deliver(direct, held_pot, held_filtered, potential_ref, filtered_ref, buf, pot_buf, in_sem, out_sem):
    norb = held_filtered.shape[0]
    if direct:
        puts = [pltpu.make_async_copy(held_pot, potential_ref, out_sem.at[norb])]
        puts += [pltpu.make_async_copy(held_filtered.at[i], filtered_ref.at[i], out_sem.at[i]) for i in range(norb)]
        for put in puts:
            put.start()
    else:
        gets = [pltpu.make_async_copy(held_pot, pot_buf, in_sem.at[norb])]
        gets += [pltpu.make_async_copy(held_filtered.at[i], buf.at[i], in_sem.at[i]) for i in range(norb)]
        puts = [pltpu.make_async_copy(pot_buf, potential_ref, out_sem.at[norb])]
        puts += [pltpu.make_async_copy(buf.at[i], filtered_ref.at[i], out_sem.at[i]) for i in range(norb)]
        for get in gets:
            get.start()
        for get, put in zip(gets, puts):
            get.wait()
            put.start()
    for put in puts:
        put.wait()


def fast(count_band, count_dom, orbitals, occupation, dielectric, core_density, start_field):
    norb, planes, rows, lanes = orbitals.shape
    per = norb // count_dom
    tall = count_dom * planes
    extent = planes + 2 * ITERS
    high = rows + 16
    chips = count_dom // 2

    def vmem(*shape):
        return pltpu.VMEM(shape, jnp.float32)

    def dma(*shape):
        return pltpu.SemaphoreType.DMA(shape)

    parts = planes // 3
    scratch = [
        vmem(norb, planes, rows, lanes),
        pltpu.SMEM((norb,), jnp.float32),
        vmem(planes, rows, lanes),
        vmem(planes, rows, lanes),
        vmem(planes, rows, lanes),
        vmem(planes, rows, lanes),
        vmem(planes, rows, lanes),
        vmem(planes + 2 * (ITERS - 1), rows, lanes),
        vmem(extent, high, lanes),
        vmem(ITERS + 1, extent, high, lanes),
        vmem(6, extent, rows, lanes),
        vmem(extent, rows, lanes),
        vmem(planes, rows, lanes),
        vmem(planes, rows, lanes),
        vmem(tall, rows, lanes),
        vmem(per, tall + 6, high, lanes),
        vmem(per, tall + 6, high, lanes),
        vmem(per, tall + 6, high, lanes),
        vmem(per, tall + 6, high, lanes),
        vmem(per, tall, rows, lanes),
        pltpu.VMEM((2 * lanes, lanes), jnp.bfloat16),
        vmem(DEGREE, 3, rows, lanes),
        dma(4 + per),
        dma(1),
        dma(4), dma(4),
        dma(per, count_dom), dma(per, count_dom),
        dma(planes), dma(planes),
        dma(planes), dma(planes),
        dma(planes), dma(planes),
        dma(planes),
        dma(2, ITERS - 1), dma(2, ITERS - 1),
        dma(chips), dma(chips),
        dma(chips), dma(chips),
        dma(1), dma(1),
        dma(chips, 2), dma(chips, 2),
        dma(per, count_dom, parts), dma(per, count_dom, parts),
        dma(1 + per * parts),
    ]

    def kernel(*refs):
        exchange(count_band, count_dom, refs[:5], refs[5], refs[6], refs[7:])

    hbm = pl.BlockSpec(memory_space=pl.ANY)

    def pin(array):
        return pltpu.with_memory_space_constraint(array, pltpu.HBM)

    held = pl.pallas_call(
        kernel,
        out_shape=(
            jax.ShapeDtypeStruct((planes, rows, lanes), jnp.float32),
            jax.ShapeDtypeStruct(orbitals.shape, jnp.float32),
        ),
        in_specs=[hbm] * 5,
        out_specs=(hbm, hbm),
        scratch_shapes=scratch,
        compiler_params=pltpu.CompilerParams(
            collective_id=0, has_side_effects=True, vmem_limit_bytes=40 * 1024 * 1024
        ),
        name="filter_whole",
    )(pin(orbitals), pin(occupation), pin(dielectric), pin(core_density), pin(start_field))
    hold = (planes, rows, lanes) if not True else (8, 8, 128)
    return pl.pallas_call(
        functools.partial(deliver, True),
        out_shape=(
            jax.ShapeDtypeStruct((planes, rows, lanes), jnp.float32),
            jax.ShapeDtypeStruct(orbitals.shape, jnp.float32),
        ),
        in_specs=[hbm, hbm],
        out_specs=(hbm, hbm),
        scratch_shapes=[vmem(norb, *hold), vmem(*hold), dma(norb + 1), dma(norb + 1)],
        compiler_params=pltpu.CompilerParams(vmem_limit_bytes=16 * 1024 * 1024),
        name="deliver",
    )(*held)


def program(count_band, count_dom, *arrays):
    norb, planes, rows, lanes = arrays[0].shape
    suits = (
        norb % count_dom == 0
        and count_dom % 4 == 0
        and count_dom > 2
        and count_band % 2 == 0
        and planes >= ITERS
        and planes % 6 == 0
        and rows % 8 == 0
        and lanes == 128
    )
    if suits:
        return fast(count_band, count_dom, *arrays)
    return local(*arrays)


def solution(mesh):
    return jax.shard_map(
        functools.partial(program, mesh.shape["band"], mesh.shape["dom"]),
        mesh=mesh,
        in_specs=(
            P("band", "dom", None, None),
            P("band"),
            P("dom", None, None),
            P("dom", None, None),
            P("dom", None, None),
        ),
        out_specs=(P("dom", None, None), P("band", "dom", None, None)),
        check_vma=False,
    )
```

```python
import functools

import jax
import jax.numpy as jnp
from jax import lax
from jax.experimental import pallas as pl
from jax.experimental.pallas import tpu as pltpu
from jax.sharding import PartitionSpec as P

ITERS = 4
DEGREE = 4


coeff_one = 1.5
coeff_two = -0.15
coeff_three = 1.0 / 90.0
coeff_zero = -49.0 / 18.0
center_value = 5.25
half_value = 4.75
slater = -0.9847450218426964


def padded_2(cells, sides, width):
    for axis, dim in sides:
        count = lax.axis_size(axis)
        ends = count - 1
        head = lax.slice_in_dim(cells, 0, width, axis=dim)
        tail = lax.slice_in_dim(cells, cells.shape[dim] - width, cells.shape[dim], axis=dim)
        cells = jnp.concatenate(
            [
                lax.ppermute(tail, axis, [(i, (i + 1) % count) for i in range(ends)]),
                cells,
                lax.ppermute(head, axis, [((i + 1) % count, i) for i in range(ends)]),
            ],
            axis=dim,
        )
    return cells


def laplace(padded):
    size_x = padded.shape[-3] - 6
    size_y = padded.shape[-2] - 6
    size_z = padded.shape[-1] - 6
    core = padded[..., 3 : 3 + size_x, 3 : 3 + size_y, 3 : 3 + size_z]
    total = 3.0 * coeff_zero * core
    for dist, weight in ((1, coeff_one), (2, coeff_two), (3, coeff_three)):
        along = padded[..., 3 + dist : 3 + dist + size_x, 3 : 3 + size_y, 3 : 3 + size_z]
        along = along + padded[..., 3 - dist : 3 - dist + size_x, 3 : 3 + size_y, 3 : 3 + size_z]
        along = along + padded[..., 3 : 3 + size_x, 3 + dist : 3 + dist + size_y, 3 : 3 + size_z]
        along = along + padded[..., 3 : 3 + size_x, 3 - dist : 3 - dist + size_y, 3 : 3 + size_z]
        along = along + padded[..., 3 : 3 + size_x, 3 : 3 + size_y, 3 + dist : 3 + dist + size_z]
        along = along + padded[..., 3 : 3 + size_x, 3 : 3 + size_y, 3 - dist : 3 - dist + size_z]
        total = total + weight * along
    return total


def face_weights(permit, padded):
    weights = (
        0.5 * (permit + padded[2:, 1:-1, 1:-1]),
        0.5 * (permit + padded[:-2, 1:-1, 1:-1]),
        0.5 * (permit + padded[1:-1, 2:, 1:-1]),
        0.5 * (permit + padded[1:-1, :-2, 1:-1]),
        0.5 * (permit + padded[1:-1, 1:-1, 2:]),
        0.5 * (permit + padded[1:-1, 1:-1, :-2]),
    )
    denominator = weights[0] + weights[1] + weights[2] + weights[3] + weights[4] + weights[5]
    return (weights, denominator)


def sweep(padded, weights, denominator, source):
    numerator = weights[0] * padded[2:, 1:-1, 1:-1] + weights[1] * padded[:-2, 1:-1, 1:-1]
    numerator = (
        numerator + weights[2] * padded[1:-1, 2:, 1:-1] + weights[3] * padded[1:-1, :-2, 1:-1]
    )
    numerator = (
        numerator + weights[4] * padded[1:-1, 1:-1, 2:] + weights[5] * padded[1:-1, 1:-1, :-2]
    )
    return (numerator + source) / denominator


def copies_rim(block):
    padded = padded_2(block, (("dom", 0),), 1)
    return jnp.pad(padded, ((0, 0), (1, 1), (1, 1)))


def apply_extended(padded_x, pot):
    padded = jnp.pad(padded_x, ((0, 0), (0, 0), (3, 3), (3, 3)))
    inner = padded_x[:, 3:-3]
    return -0.5 * laplace(padded) + pot[None] * inner


def local(orbitals, occupation, dielectric, core_density, start_field):
    partial_density = jnp.sum(occupation[:, None, None, None] * orbitals * orbitals, axis=0)
    density = lax.psum(partial_density, "band")
    permit_pad = padded_2(dielectric, (("dom", 0),), 1)
    permit_pad = jnp.pad(permit_pad, ((0, 0), (1, 1), (1, 1)))
    weights, denominator = face_weights(dielectric, permit_pad)
    source = 4.0 * density
    field = start_field
    for turn_index in range(ITERS):
        field = sweep(copies_rim(field), weights, denominator, source)
    potential = field + slater * jnp.cbrt(density + core_density)

    def hamil(block):
        padded = padded_2(block, (("dom", 1),), 3)
        return apply_extended(padded, potential)

    before = orbitals
    current = (hamil(orbitals) - center_value * orbitals) / half_value
    for turn_index in range(DEGREE - 1):
        nextone = 2.0 * (hamil(current) - center_value * current) / half_value - before
        before = current
        current = nextone
    return (potential, current)


MESH = pl.DeviceIdType.MESH
FEEDS = (5, 6, 14)
SWAP_AHEAD = 2


def exchange(count_band, count_dom, refs_in, potential_ref, filtered_ref, scratch):
    orbitals_ref, occupation_ref, dielectric_ref, core_ref, start_ref = refs_in
    (
        orbs, share, own, part_in, side, other, acc, density, eps, fields, weights, inverse,
        core, pot_own, strength, wave, later_one, later_two, later_three, result, stripes, sums,
        load_sem, share_sem, halo_send, halo_recv, in_send, in_recv, acc_send, acc_recv,
        side_send, side_recv, other_send, other_recv, relay_send,
        den_send, den_recv, pot_send, pot_recv, swap_send, swap_recv, mate_send, mate_recv, pass_send, pass_recv, out_send, out_recv, end_sem,
    ) = scratch
    later = (later_one, later_two, later_three)
    norb, planes, rows, lanes = orbitals_ref.shape
    per = norb // count_dom
    wide = 8
    reach = 3
    band = lax.axis_index("band")
    dom = lax.axis_index("dom")
    middle = count_band // 2
    in_left = band < middle
    toward = jnp.where(in_left, 1, -1)
    inner = band + toward
    outer = band - toward
    has_outer = jnp.logical_and(band > 0, band < count_band - 1)
    is_mid = jnp.logical_or(band == middle - 1, band == middle)
    has_left = dom > 0
    has_right = dom < count_dom - 1
    partner = dom + 1 - 2 * lax.rem(dom, 2)
    body = pl.ds(wide, rows)
    half = planes // 2
    chips = count_dom // 2
    odd = lax.rem(band, 2)
    mate = band + 1 - 2 * odd
    shift = odd * half

    def peer(step):
        return lax.rem(dom + step, count_dom)

    def remote(src, dst, send, recv, **where):
        return pltpu.make_async_remote_copy(
            src_ref=src, dst_ref=dst, send_sem=send, recv_sem=recv, device_id=where, device_id_type=MESH
        )

    loads = [
        pltpu.make_async_copy(orbitals_ref, orbs, load_sem.at[0]),
        pltpu.make_async_copy(dielectric_ref, eps.at[pl.ds(ITERS, planes), body], load_sem.at[1]),
        pltpu.make_async_copy(start_ref, fields.at[0, pl.ds(ITERS, planes), body], load_sem.at[2]),
        pltpu.make_async_copy(core_ref, core, load_sem.at[3]),
    ]
    for index in range(per):
        loads.append(
            pltpu.make_async_copy(
                orbitals_ref.at[dom * per + index],
                wave.at[index, pl.ds(reach + dom * planes, planes), body],
                load_sem.at[4 + index],
            )
        )
    shares = pltpu.make_async_copy(occupation_ref, share, share_sem.at[0])
    shares.start()
    for copy in loads:
        copy.start()

    barrier = pltpu.get_barrier_semaphore()
    for step in range(1, count_dom):
        pl.semaphore_signal(barrier, inc=1, device_id={"dom": peer(step)}, device_id_type=MESH)
    pl.semaphore_signal(barrier, inc=1, device_id={"band": inner}, device_id_type=MESH)
    pl.semaphore_signal(barrier, inc=1, device_id={"band": band + 1 - 2 * lax.rem(band, 2)}, device_id_type=MESH)

    @pl.when(has_outer)
    def _():
        pl.semaphore_signal(barrier, inc=1, device_id={"band": outer}, device_id_type=MESH)

    def clear_rows(ref, index):
        ref[index, :wide, :] = jnp.zeros((wide, lanes), jnp.float32)
        ref[index, wide + rows :, :] = jnp.zeros((wide, lanes), jnp.float32)

    def clear_plane(ref, index):
        ref[index] = jnp.zeros(ref.shape[1:], jnp.float32)

    extent = planes + 2 * ITERS
    tall = count_dom * planes
    pl.semaphore_wait(barrier, count_dom + 1 + jnp.where(has_outer, 1, 0))

    reserve = max(ITERS - half, 1)

    def halo(source, target, index, deep_left):
        from_left, from_right = (ITERS, reserve) if deep_left else (reserve, ITERS)
        right = remote(
            source.at[pl.ds(planes - from_left, from_left)], target.at[pl.ds(ITERS - from_left, from_left), body],
            halo_send.at[index], halo_recv.at[index], dom=dom + 1,
        )
        left = remote(
            source.at[pl.ds(0, from_right)], target.at[pl.ds(ITERS + planes, from_right), body],
            halo_send.at[index + 1], halo_recv.at[index + 1], dom=dom - 1,
        )
        return right, left

    depth = ITERS - 1

    def den(plane, right):
        spot = plane - (planes - depth) if right else plane
        here = density.at[depth + plane]
        there = density.at[spot] if right else density.at[depth + planes + spot]
        way = 0 if right else 1
        return remote(
            here, there, den_send.at[way, spot], den_recv.at[way, spot], dom=dom + 1 if right else dom - 1
        )

    def sides(start):
        for parity in range(2):
            for here, mine, theirs in ((has_right, 0, 1), (has_left, 1, 0)):
                @pl.when(jnp.logical_and(odd == parity, here))
                def _(parity=parity, mine=mine, theirs=theirs):
                    for source, target, index in ((dielectric_ref, eps, 0), (start_ref, fields.at[0], 2)):
                        pair = halo(source, target, index, parity == 0)
                        if start:
                            pair[mine].start()
                        else:
                            pair[mine].wait_send()
                            pair[theirs].wait_recv()

    sides(True)

    def incoming(index, step):
        return remote(
            orbitals_ref.at[peer(step) * per + index],
            wave.at[index, pl.ds(reach + dom * planes, planes), body],
            in_send.at[index], in_recv.at[index], dom=peer(step),
        )

    def arrived(index, send, recv):
        here = result.at[index, pl.ds(0, tall - planes)]
        return remote(here, wave.at[index, pl.ds(reach, tall - planes), body], send.at[index], recv.at[index], dom=partner)

    bulk = [(index, step) for index in range(per) for step in range(1, count_dom)]

    def feed(start, stop):
        for index, step in bulk[start:stop]:
            incoming(index, step).start()

    held = lax.rem(dom + band, 2) == 1
    feed(0, FEEDS[0])

    @pl.when(jnp.logical_not(held))
    def _():
        feed(FEEDS[0], FEEDS[1])

    shares.wait()
    loads[0].wait()

    def to_inner(plane):
        return remote(acc.at[plane], part_in.at[plane], acc_send.at[plane], acc_recv.at[plane], band=inner)

    def cross(plane):
        return remote(acc.at[plane], other.at[plane], other_send.at[plane], other_recv.at[plane], band=inner)

    def back(plane, source):
        return remote(source.at[plane], side.at[plane], side_send.at[plane], side_recv.at[plane], band=outer)

    def relay(plane):
        return remote(other.at[plane], other.at[plane], relay_send.at[plane], other_recv.at[plane], band=outer)

    @pl.loop(0, planes)
    def _(plane):
        total = jnp.zeros((rows, lanes), jnp.float32)
        for index in range(norb):
            cells = orbs[index, plane]
            total = total + share[index] * cells * cells

        @pl.when(has_outer)
        def _():
            own[plane] = total

        @pl.when(jnp.logical_not(has_outer))
        def _():
            acc[plane] = total

            @pl.when(is_mid)
            def _():
                cross(plane).start()

            @pl.when(jnp.logical_not(is_mid))
            def _():
                to_inner(plane).start()


    @pl.loop(0, extent)
    def _(index):
        clear_rows(eps, index)
        for turn in range(ITERS):
            clear_rows(fields.at[turn], index)

    @pl.when(jnp.logical_not(has_left))
    def _():
        for index in range(ITERS):
            eps[index, body, :] = jnp.zeros((rows, lanes), jnp.float32)
            fields[0, index, body, :] = jnp.zeros((rows, lanes), jnp.float32)
        for index in range(ITERS - 1):
            density[index] = jnp.zeros((rows, lanes), jnp.float32)

    @pl.when(jnp.logical_not(has_right))
    def _():
        for index in range(ITERS):
            eps[ITERS + planes + index, body, :] = jnp.zeros((rows, lanes), jnp.float32)
            fields[0, ITERS + planes + index, body, :] = jnp.zeros((rows, lanes), jnp.float32)
        for index in range(ITERS - 1):
            density[ITERS - 1 + planes + index] = jnp.zeros((rows, lanes), jnp.float32)

    for ref in [stack.at[index] for stack in (wave, *later) for index in range(per)]:
        for index in range(reach):
            clear_plane(ref, index)
            clear_plane(ref, reach + tall + index)

        @pl.loop(reach, reach + tall)
        def _(index, ref=ref):
            clear_rows(ref, index)

    gap = jnp.abs(
        lax.broadcasted_iota(jnp.int32, (2 * lanes, lanes), 0) % lanes
        - lax.broadcasted_iota(jnp.int32, (2 * lanes, lanes), 1)
    )
    weight = jnp.where(gap == 1, 135.0, jnp.where(gap == 2, -13.5, jnp.where(gap == 3, 1.0, 0.0)))
    stripes[...] = weight.astype(jnp.bfloat16)
    scale = -coeff_three / half_value

    @pl.when(has_outer)
    def _():
        @pl.loop(0, planes)
        def _(plane):
            to_inner(plane).wait_recv()
            acc[plane] = own[plane] + part_in[plane]

            @pl.when(is_mid)
            def _():
                cross(plane).start()
                back(plane, acc).start()

            @pl.when(jnp.logical_not(is_mid))
            def _():
                to_inner(plane).start()

    def settle():
        loads[1].wait()
        loads[2].wait()
        loads[3].wait()
        sides(False)
        lane = lax.broadcasted_iota(jnp.int32, (rows, lanes), 1)
        row = lax.broadcasted_iota(jnp.int32, (rows, lanes), 0)
        zero = jnp.zeros((rows, lanes), jnp.float32)

        @pl.loop(0, half + 2 * depth)
        def _(spot):
            index = 1 + shift + spot
            here = eps[index, body, :]
            ahead = jnp.where(lane < lanes - 1, pltpu.roll(here, lanes - 1, 1), zero)
            behind = jnp.where(lane > 0, pltpu.roll(here, 1, 1), zero)
            faces = (
                0.5 * (here + eps[index + 1, body, :]),
                0.5 * (here + eps[index - 1, body, :]),
                0.5 * (here + eps[index, wide + 1 : wide + 1 + rows, :]),
                0.5 * (here + eps[index, wide - 1 : wide - 1 + rows, :]),
                0.5 * (here + ahead),
                0.5 * (here + behind),
            )
            denominator = faces[0] + faces[1] + faces[2] + faces[3] + faces[4] + faces[5]
            cell = dom * planes + index - ITERS
            inside = jnp.logical_and(cell >= 0, cell < tall)
            factor = jnp.where(inside, 1.0 / jnp.where(inside, denominator, 1.0), zero)
            inverse[index] = 4.0 * factor
            for face in range(4):
                weights[face, index] = faces[face] * factor
            weights[4, index] = jnp.where(lane < lanes - 1, faces[4] * factor, zero)
            weights[5, index] = jnp.where(lane > 0, faces[5] * factor, zero)

    pl.when(jnp.logical_not(is_mid))(settle)

    @pl.loop(0, planes)
    def _(plane):
        @pl.when(jnp.logical_not(is_mid))
        def _():
            back(plane, side).wait_recv()

            @pl.when(has_outer)
            def _():
                back(plane, side).start()

        cross(plane).wait_recv()

        @pl.when(has_outer)
        def _():
            relay(plane).start()

        @pl.when(is_mid)
        def _():
            density[depth + plane] = acc[plane] + other[plane]

        @pl.when(jnp.logical_not(is_mid))
        def _():
            density[depth + plane] = side[plane] + other[plane]

        @pl.when(jnp.logical_and(jnp.logical_and(odd == 0, has_right), plane >= planes - depth))
        def _():
            den(plane, True).start()

        @pl.when(jnp.logical_and(jnp.logical_and(odd == 1, has_left), plane < depth))
        def _():
            den(plane, False).start()

    pl.when(is_mid)(settle)

    @pl.when(held)
    def _():
        feed(FEEDS[0], FEEDS[1])

    def sweep_at(turn, index):
        before, after = fields.at[turn], fields.at[turn + 1]
        here = before[index, body, :]
        total = density[index - 1] * inverse[index]
        total = total + (
            weights[0, index] * before[index + 1, body, :] + weights[1, index] * before[index - 1, body, :]
        )
        total = total + (
            weights[2, index] * before[index, wide + 1 : wide + 1 + rows, :]
            + weights[3, index] * before[index, wide - 1 : wide - 1 + rows, :]
        )
        total = total + (
            weights[4, index] * pltpu.roll(here, lanes - 1, 1) + weights[5, index] * pltpu.roll(here, 1, 1)
        )
        after[index, body, :] = total

    for turn in range(ITERS - 1):
        first = turn + jnp.where(odd == 0, ITERS, 1 + half)
        for spot in range(half + depth - 2 * turn):
            sweep_at(turn, first + spot)

    @pl.when(jnp.logical_and(odd == 0, has_left))
    def _():
        for spot in range(depth):
            den(planes - depth + spot, True).wait_recv()

    @pl.when(jnp.logical_and(odd == 1, has_right))
    def _():
        for spot in range(depth):
            den(spot, False).wait_recv()

    for turn in range(ITERS - 1):
        first = jnp.where(odd == 0, 1 + turn, ITERS + planes - turn)
        for spot in range(depth):
            sweep_at(turn, first + spot)

    def potential_at(plane):
        sweep_at(ITERS - 1, ITERS + plane)
        cells = density[depth + plane] + core[plane]
        root = jnp.exp(jnp.log(cells) * (1.0 / 3.0))
        root = root - (root - cells / (root * root)) * (1.0 / 3.0)
        pot = fields[ITERS, ITERS + plane, body, :] + slater * root
        pot_own[plane] = pot
        strength[dom * planes + plane] = (pot - (center_value + 1.5 * coeff_zero)) * (2.0 / half_value)

    mine = pl.ds(dom * planes, planes)

    def piece(step, which):
        return pl.ds(lax.rem(dom + count_dom - 2 * step, count_dom) * planes + which * half, half)

    near = jnp.where(lax.rem(dom // 2, 2) == 0, chips - 1, 1)
    order = [near] + [2 * pair for pair in range(1, chips // 2)]
    order += [lax.rem(near + 2 * pair, chips) for pair in range(1, chips // 2)]

    def spread(step):
        here = strength.at[piece(0, odd)]
        return remote(here, here, pot_send.at[step], pot_recv.at[step], dom=peer(2 * step))

    def share_pot():
        here = pot_own.at[pl.ds(shift, half)]
        return remote(here, here, mate_send.at[0], mate_recv.at[0], band=mate)

    def swap(step):
        here = strength.at[piece(step, odd)]
        return remote(here, here, swap_send.at[step], swap_recv.at[step], band=mate)

    def hand(step, late):
        here = strength.at[piece(step, 1 - odd if late else odd)]
        return remote(here, here, pass_send.at[step, late], pass_recv.at[step, late], dom=partner)

    @pl.loop(0, half)
    def _(spot):
        potential_at(shift + spot)

    for step in order:
        spread(chips - step).start()
    swap(0).start()
    hand(0, 0).start()
    share_pot().start()
    feed(FEEDS[1], FEEDS[2])

    def pass_on(step):
        spread(step).wait_recv()
        swap(step).start()
        hand(step, 0).start()

    for step in order[: chips // 2]:
        pass_on(step)
    swap(0).wait_recv()
    hand(0, 1).start()
    feed(FEEDS[2], len(bulk))
    for step in order[chips // 2 :]:
        pass_on(step)

    units = tall // reach
    parts = planes // reach
    span = 2 * parts
    origin = (dom // 2) * span

    levels = (wave, *later)

    def place(level, tick):
        spot = jnp.maximum(tick - 3 * level, 0)
        return jnp.minimum(spot // units, per - 1), lax.rem(origin + level + spot, units)

    def advance(tick):
        places = [place(level, tick) for level in range(DEGREE)]
        sources = [levels[level].at[places[level][0]] for level in range(DEGREE)]
        cells = jnp.concatenate(
            [
                sources[level][pl.ds(reach + places[level][1] * reach, reach), body, :].reshape(reach * rows, lanes)
                for level in range(DEGREE)
            ],
            axis=0,
        )
        high = cells.astype(jnp.bfloat16)
        rest = cells - high.astype(jnp.float32)
        mid = rest.astype(jnp.bfloat16)
        low = (rest - mid.astype(jnp.float32)).astype(jnp.bfloat16)
        lines = jnp.dot(
            jnp.concatenate([high, mid], axis=1), stripes[...], preferred_element_type=jnp.float32
        ) + jnp.dot(low, stripes[:lanes], preferred_element_type=jnp.float32)
        sums[...] = lines.reshape(DEGREE, reach, rows, lanes)
        for level in reversed(range(DEGREE)):
            index, unit = places[level]
            ref = sources[level]
            for local_plane in range(reach):
                at = unit * reach + local_plane
                here = ref[reach + at, body, :]

                def around(dist):
                    along = ref[reach + at + dist, body, :] + ref[reach + at - dist, body, :]
                    return along + (
                        ref[reach + at, wide + dist : wide + dist + rows, :]
                        + ref[reach + at, wide - dist : wide - dist + rows, :]
                    )

                total = sums[level, local_plane] + around(3)
                total = total + 135.0 * around(1) - 13.5 * around(2)
                value = strength[at] * here + scale * total
                if level == 0:
                    value = 0.5 * value
                else:
                    value = value - levels[level - 1][index, reach + at, body, :]
                if level < DEGREE - 1:
                    levels[level + 1][index, reach + at, body, :] = value
                else:
                    result[index, at] = value

    def leave(index, unit):
        block = unit // parts
        step = lax.rem(block - dom + count_dom, count_dom)
        part = lax.rem(unit, parts)
        here = result.at[index, pl.ds(unit * reach, reach)]
        there = filtered_ref.at[dom * per + index, pl.ds(part * reach, reach)]
        away = remote(here, there, out_send.at[index], out_recv.at[index], dom=block)
        return step, away, pltpu.make_async_copy(here, there, end_sem.at[1 + index * parts + part])

    hand(0, 0).wait_recv()
    hand(0, 1).wait_recv()

    @pl.loop(0, per * units + 3 * (DEGREE - 1))
    def _(tick):
        @pl.when(jnp.logical_and(lax.rem(tick, units) == 0, tick < per * units))
        def _():
            index = tick // units
            pltpu.make_async_copy(
                orbitals_ref.at[dom * per + index],
                wave.at[index, pl.ds(reach + dom * planes, planes), body],
                load_sem.at[4 + index],
            ).wait()
            arrived(index, in_send, in_recv).wait_recv()

        for ahead in range(1, chips):
            @pl.when(tick == ahead * span - SWAP_AHEAD)
            def _(step=chips - ahead):
                swap(step).wait_recv()
                hand(step, 1).start()

            @pl.when(tick == ahead * span)
            def _(step=chips - ahead):
                hand(step, 0).wait_recv()
                hand(step, 1).wait_recv()

        advance(tick)

        @pl.when(tick >= 3 * (DEGREE - 1))
        def _():
            step, away, home = leave(*place(DEGREE - 1, tick))

            @pl.when(step > 0)
            def _():
                away.start()

            @pl.when(step == 0)
            def _():
                home.start()

    share_pot().wait()
    keep = pltpu.make_async_copy(pot_own, potential_ref, end_sem.at[0])
    keep.start()
    for step in range(1, chips):
        spread(step).wait_send()
    for step in range(chips):
        swap(step).wait_send()
        hand(step, 0).wait_send()
        hand(step, 1).wait_send()
    for index in range(per):
        arrived(index, in_send, in_recv).wait_send()

    @pl.loop(0, planes)
    def _(plane):
        @pl.when(is_mid)
        def _():
            cross(plane).wait_send()

        @pl.when(jnp.logical_not(is_mid))
        def _():
            to_inner(plane).wait_send()

        @pl.when(has_outer)
        def _():
            back(plane, acc).wait_send()
            relay(plane).wait_send()

        @pl.when(jnp.logical_and(jnp.logical_and(odd == 0, has_right), plane >= planes - depth))
        def _():
            den(plane, True).wait_send()

        @pl.when(jnp.logical_and(jnp.logical_and(odd == 1, has_left), plane < depth))
        def _():
            den(plane, False).wait_send()

    keep.wait()
    for index in range(per):
        for part in range(parts):
            leave(index, dom * parts + part)[2].wait()
        arrived(index, out_send, out_recv).wait()


def deliver(direct, held_pot, held_filtered, potential_ref, filtered_ref, buf, pot_buf, in_sem, out_sem):
    norb = held_filtered.shape[0]
    if direct:
        puts = [pltpu.make_async_copy(held_pot, potential_ref, out_sem.at[norb])]
        puts += [pltpu.make_async_copy(held_filtered.at[i], filtered_ref.at[i], out_sem.at[i]) for i in range(norb)]
        for put in puts:
            put.start()
    else:
        gets = [pltpu.make_async_copy(held_pot, pot_buf, in_sem.at[norb])]
        gets += [pltpu.make_async_copy(held_filtered.at[i], buf.at[i], in_sem.at[i]) for i in range(norb)]
        puts = [pltpu.make_async_copy(pot_buf, potential_ref, out_sem.at[norb])]
        puts += [pltpu.make_async_copy(buf.at[i], filtered_ref.at[i], out_sem.at[i]) for i in range(norb)]
        for get in gets:
            get.start()
        for get, put in zip(gets, puts):
            get.wait()
            put.start()
    for put in puts:
        put.wait()


def fast(count_band, count_dom, orbitals, occupation, dielectric, core_density, start_field):
    norb, planes, rows, lanes = orbitals.shape
    per = norb // count_dom
    tall = count_dom * planes
    extent = planes + 2 * ITERS
    high = rows + 16
    chips = count_dom // 2

    def vmem(*shape):
        return pltpu.VMEM(shape, jnp.float32)

    def dma(*shape):
        return pltpu.SemaphoreType.DMA(shape)

    parts = planes // 3
    scratch = [
        vmem(norb, planes, rows, lanes),
        pltpu.SMEM((norb,), jnp.float32),
        vmem(planes, rows, lanes),
        vmem(planes, rows, lanes),
        vmem(planes, rows, lanes),
        vmem(planes, rows, lanes),
        vmem(planes, rows, lanes),
        vmem(planes + 2 * (ITERS - 1), rows, lanes),
        vmem(extent, high, lanes),
        vmem(ITERS + 1, extent, high, lanes),
        vmem(6, extent, rows, lanes),
        vmem(extent, rows, lanes),
        vmem(planes, rows, lanes),
        vmem(planes, rows, lanes),
        vmem(tall, rows, lanes),
        vmem(per, tall + 6, high, lanes),
        vmem(per, tall + 6, high, lanes),
        vmem(per, tall + 6, high, lanes),
        vmem(per, tall + 6, high, lanes),
        vmem(per, tall, rows, lanes),
        pltpu.VMEM((2 * lanes, lanes), jnp.bfloat16),
        vmem(DEGREE, 3, rows, lanes),
        dma(4 + per),
        dma(1),
        dma(4), dma(4),
        dma(per), dma(per),
        dma(planes), dma(planes),
        dma(planes), dma(planes),
        dma(planes), dma(planes),
        dma(planes),
        dma(2, ITERS - 1), dma(2, ITERS - 1),
        dma(chips), dma(chips),
        dma(chips), dma(chips),
        dma(1), dma(1),
        dma(chips, 2), dma(chips, 2),
        dma(per), dma(per),
        dma(1 + per * parts),
    ]

    def kernel(*refs):
        exchange(count_band, count_dom, refs[:5], refs[5], refs[6], refs[7:])

    hbm = pl.BlockSpec(memory_space=pl.ANY)

    def pin(array):
        return pltpu.with_memory_space_constraint(array, pltpu.HBM)

    held = pl.pallas_call(
        kernel,
        out_shape=(
            jax.ShapeDtypeStruct((planes, rows, lanes), jnp.float32),
            jax.ShapeDtypeStruct(orbitals.shape, jnp.float32),
        ),
        in_specs=[hbm] * 5,
        out_specs=(hbm, hbm),
        scratch_shapes=scratch,
        compiler_params=pltpu.CompilerParams(
            collective_id=0, has_side_effects=True, vmem_limit_bytes=40 * 1024 * 1024
        ),
        name="filter_whole",
    )(pin(orbitals), pin(occupation), pin(dielectric), pin(core_density), pin(start_field))
    hold = (planes, rows, lanes) if not True else (8, 8, 128)
    return pl.pallas_call(
        functools.partial(deliver, True),
        out_shape=(
            jax.ShapeDtypeStruct((planes, rows, lanes), jnp.float32),
            jax.ShapeDtypeStruct(orbitals.shape, jnp.float32),
        ),
        in_specs=[hbm, hbm],
        out_specs=(hbm, hbm),
        scratch_shapes=[vmem(norb, *hold), vmem(*hold), dma(norb + 1), dma(norb + 1)],
        compiler_params=pltpu.CompilerParams(vmem_limit_bytes=16 * 1024 * 1024),
        name="deliver",
    )(*held)


def program(count_band, count_dom, *arrays):
    norb, planes, rows, lanes = arrays[0].shape
    suits = (
        norb % count_dom == 0
        and count_dom % 4 == 0
        and count_dom > 2
        and count_band % 2 == 0
        and planes >= ITERS
        and planes % 6 == 0
        and rows % 8 == 0
        and lanes == 128
    )
    if suits:
        return fast(count_band, count_dom, *arrays)
    return local(*arrays)


def solution(mesh):
    return jax.shard_map(
        functools.partial(program, mesh.shape["band"], mesh.shape["dom"]),
        mesh=mesh,
        in_specs=(
            P("band", "dom", None, None),
            P("band"),
            P("dom", None, None),
            P("dom", None, None),
            P("dom", None, None),
        ),
        out_specs=(P("dom", None, None), P("band", "dom", None, None)),
        check_vma=False,
    )
```

```python
import functools

import jax
import jax.numpy as jnp
from jax import lax
from jax.experimental import pallas as pl
from jax.experimental.pallas import tpu as pltpu
from jax.sharding import PartitionSpec as P

ITERS = 4
DEGREE = 4


coeff_one = 1.5
coeff_two = -0.15
coeff_three = 1.0 / 90.0
coeff_zero = -49.0 / 18.0
center_value = 5.25
half_value = 4.75
slater = -0.9847450218426964


def padded_2(cells, sides, width):
    for axis, dim in sides:
        count = lax.axis_size(axis)
        ends = count - 1
        head = lax.slice_in_dim(cells, 0, width, axis=dim)
        tail = lax.slice_in_dim(cells, cells.shape[dim] - width, cells.shape[dim], axis=dim)
        cells = jnp.concatenate(
            [
                lax.ppermute(tail, axis, [(i, (i + 1) % count) for i in range(ends)]),
                cells,
                lax.ppermute(head, axis, [((i + 1) % count, i) for i in range(ends)]),
            ],
            axis=dim,
        )
    return cells


def laplace(padded):
    size_x = padded.shape[-3] - 6
    size_y = padded.shape[-2] - 6
    size_z = padded.shape[-1] - 6
    core = padded[..., 3 : 3 + size_x, 3 : 3 + size_y, 3 : 3 + size_z]
    total = 3.0 * coeff_zero * core
    for dist, weight in ((1, coeff_one), (2, coeff_two), (3, coeff_three)):
        along = padded[..., 3 + dist : 3 + dist + size_x, 3 : 3 + size_y, 3 : 3 + size_z]
        along = along + padded[..., 3 - dist : 3 - dist + size_x, 3 : 3 + size_y, 3 : 3 + size_z]
        along = along + padded[..., 3 : 3 + size_x, 3 + dist : 3 + dist + size_y, 3 : 3 + size_z]
        along = along + padded[..., 3 : 3 + size_x, 3 - dist : 3 - dist + size_y, 3 : 3 + size_z]
        along = along + padded[..., 3 : 3 + size_x, 3 : 3 + size_y, 3 + dist : 3 + dist + size_z]
        along = along + padded[..., 3 : 3 + size_x, 3 : 3 + size_y, 3 - dist : 3 - dist + size_z]
        total = total + weight * along
    return total


def face_weights(permit, padded):
    weights = (
        0.5 * (permit + padded[2:, 1:-1, 1:-1]),
        0.5 * (permit + padded[:-2, 1:-1, 1:-1]),
        0.5 * (permit + padded[1:-1, 2:, 1:-1]),
        0.5 * (permit + padded[1:-1, :-2, 1:-1]),
        0.5 * (permit + padded[1:-1, 1:-1, 2:]),
        0.5 * (permit + padded[1:-1, 1:-1, :-2]),
    )
    denominator = weights[0] + weights[1] + weights[2] + weights[3] + weights[4] + weights[5]
    return (weights, denominator)


def sweep(padded, weights, denominator, source):
    numerator = weights[0] * padded[2:, 1:-1, 1:-1] + weights[1] * padded[:-2, 1:-1, 1:-1]
    numerator = (
        numerator + weights[2] * padded[1:-1, 2:, 1:-1] + weights[3] * padded[1:-1, :-2, 1:-1]
    )
    numerator = (
        numerator + weights[4] * padded[1:-1, 1:-1, 2:] + weights[5] * padded[1:-1, 1:-1, :-2]
    )
    return (numerator + source) / denominator


def copies_rim(block):
    padded = padded_2(block, (("dom", 0),), 1)
    return jnp.pad(padded, ((0, 0), (1, 1), (1, 1)))


def apply_extended(padded_x, pot):
    padded = jnp.pad(padded_x, ((0, 0), (0, 0), (3, 3), (3, 3)))
    inner = padded_x[:, 3:-3]
    return -0.5 * laplace(padded) + pot[None] * inner


def local(orbitals, occupation, dielectric, core_density, start_field):
    partial_density = jnp.sum(occupation[:, None, None, None] * orbitals * orbitals, axis=0)
    density = lax.psum(partial_density, "band")
    permit_pad = padded_2(dielectric, (("dom", 0),), 1)
    permit_pad = jnp.pad(permit_pad, ((0, 0), (1, 1), (1, 1)))
    weights, denominator = face_weights(dielectric, permit_pad)
    source = 4.0 * density
    field = start_field
    for turn_index in range(ITERS):
        field = sweep(copies_rim(field), weights, denominator, source)
    potential = field + slater * jnp.cbrt(density + core_density)

    def hamil(block):
        padded = padded_2(block, (("dom", 1),), 3)
        return apply_extended(padded, potential)

    before = orbitals
    current = (hamil(orbitals) - center_value * orbitals) / half_value
    for turn_index in range(DEGREE - 1):
        nextone = 2.0 * (hamil(current) - center_value * current) / half_value - before
        before = current
        current = nextone
    return (potential, current)


MESH = pl.DeviceIdType.MESH
FEEDS = (5, 6, 14)
SWAP_AHEAD = 2


def exchange(count_band, count_dom, refs_in, potential_ref, filtered_ref, scratch):
    orbitals_ref, occupation_ref, dielectric_ref, core_ref, start_ref = refs_in
    (
        orbs, share, own, part_in, side, other, acc, density, eps, fields, weights, inverse,
        core, pot_own, strength, wave, later_one, later_two, later_three, result, stripes, sums,
        load_sem, share_sem, halo_send, halo_recv, in_send, in_recv, acc_send, acc_recv,
        side_send, side_recv, other_send, other_recv, relay_send,
        den_send, den_recv, pot_send, pot_recv, swap_send, swap_recv, mate_send, mate_recv, pass_send, pass_recv, out_send, out_recv, end_sem,
    ) = scratch
    later = (later_one, later_two, later_three)
    norb, planes, rows, lanes = orbitals_ref.shape
    per = norb // count_dom
    wide = 8
    reach = 3
    band = lax.axis_index("band")
    dom = lax.axis_index("dom")
    middle = count_band // 2
    in_left = band < middle
    toward = jnp.where(in_left, 1, -1)
    inner = band + toward
    outer = band - toward
    has_outer = jnp.logical_and(band > 0, band < count_band - 1)
    is_mid = jnp.logical_or(band == middle - 1, band == middle)
    has_left = dom > 0
    has_right = dom < count_dom - 1
    partner = dom + 1 - 2 * lax.rem(dom, 2)
    body = pl.ds(wide, rows)
    half = planes // 2
    chips = count_dom // 2
    odd = lax.rem(band, 2)
    mate = band + 1 - 2 * odd
    shift = odd * half

    def peer(step):
        return lax.rem(dom + step, count_dom)

    def remote(src, dst, send, recv, **where):
        return pltpu.make_async_remote_copy(
            src_ref=src, dst_ref=dst, send_sem=send, recv_sem=recv, device_id=where, device_id_type=MESH
        )

    loads = [
        pltpu.make_async_copy(orbitals_ref, orbs, load_sem.at[0]),
        pltpu.make_async_copy(dielectric_ref, eps.at[pl.ds(ITERS, planes), body], load_sem.at[1]),
        pltpu.make_async_copy(start_ref, fields.at[0, pl.ds(ITERS, planes), body], load_sem.at[2]),
        pltpu.make_async_copy(core_ref, core, load_sem.at[3]),
    ]
    for index in range(per):
        loads.append(
            pltpu.make_async_copy(
                orbitals_ref.at[dom * per + index],
                wave.at[index, pl.ds(reach + dom * planes, planes), body],
                load_sem.at[4 + index],
            )
        )
    barrier = pltpu.get_barrier_semaphore()
    for step in range(1, count_dom):
        pl.semaphore_signal(barrier, inc=1, device_id={"dom": peer(step)}, device_id_type=MESH)
    pl.semaphore_signal(barrier, inc=1, device_id={"band": inner}, device_id_type=MESH)
    pl.semaphore_signal(barrier, inc=1, device_id={"band": band + 1 - 2 * lax.rem(band, 2)}, device_id_type=MESH)

    @pl.when(has_outer)
    def _():
        pl.semaphore_signal(barrier, inc=1, device_id={"band": outer}, device_id_type=MESH)

    shares = pltpu.make_async_copy(occupation_ref, share, share_sem.at[0])
    shares.start()
    for copy in loads:
        copy.start()

    def clear_rows(ref, index):
        ref[index, :wide, :] = jnp.zeros((wide, lanes), jnp.float32)
        ref[index, wide + rows :, :] = jnp.zeros((wide, lanes), jnp.float32)

    def clear_plane(ref, index):
        ref[index] = jnp.zeros(ref.shape[1:], jnp.float32)

    extent = planes + 2 * ITERS
    tall = count_dom * planes
    pl.semaphore_wait(barrier, count_dom + 1 + jnp.where(has_outer, 1, 0))

    reserve = max(ITERS - half, 1)

    def halo(source, target, index, deep_left):
        from_left, from_right = (ITERS, reserve) if deep_left else (reserve, ITERS)
        right = remote(
            source.at[pl.ds(planes - from_left, from_left)], target.at[pl.ds(ITERS - from_left, from_left), body],
            halo_send.at[index], halo_recv.at[index], dom=dom + 1,
        )
        left = remote(
            source.at[pl.ds(0, from_right)], target.at[pl.ds(ITERS + planes, from_right), body],
            halo_send.at[index + 1], halo_recv.at[index + 1], dom=dom - 1,
        )
        return right, left

    depth = ITERS - 1

    def den(plane, right):
        spot = plane - (planes - depth) if right else plane
        here = density.at[depth + plane]
        there = density.at[spot] if right else density.at[depth + planes + spot]
        way = 0 if right else 1
        return remote(
            here, there, den_send.at[way], den_recv.at[way, spot], dom=dom + 1 if right else dom - 1
        )

    def sides(start):
        for parity in range(2):
            for here, mine, theirs in ((has_right, 0, 1), (has_left, 1, 0)):
                @pl.when(jnp.logical_and(odd == parity, here))
                def _(parity=parity, mine=mine, theirs=theirs):
                    for source, target, index in ((dielectric_ref, eps, 0), (start_ref, fields.at[0], 2)):
                        pair = halo(source, target, index, parity == 0)
                        if start:
                            pair[mine].start()
                        else:
                            pair[mine].wait_send()
                            pair[theirs].wait_recv()

    sides(True)

    def incoming(index, step):
        return remote(
            orbitals_ref.at[peer(step) * per + index],
            wave.at[index, pl.ds(reach + dom * planes, planes), body],
            in_send.at[index], in_recv.at[index], dom=peer(step),
        )

    def arrived(index, send, recv):
        here = result.at[index, pl.ds(0, tall - planes)]
        return remote(here, wave.at[index, pl.ds(reach, tall - planes), body], send.at[index], recv.at[index], dom=partner)

    bulk = [(index, step) for index in range(per) for step in range(1, count_dom)]

    def feed(start, stop):
        for index, step in bulk[start:stop]:
            incoming(index, step).start()

    held = lax.rem(dom + band, 2) == 1
    feed(0, FEEDS[0])

    @pl.when(jnp.logical_not(held))
    def _():
        feed(FEEDS[0], FEEDS[1])

    shares.wait()
    loads[0].wait()

    def to_inner(plane):
        return remote(acc.at[plane], part_in.at[plane], acc_send.at[0], acc_recv.at[plane], band=inner)

    def cross(plane):
        return remote(acc.at[plane], other.at[plane], other_send.at[0], other_recv.at[plane], band=inner)

    def back(plane, source):
        return remote(source.at[plane], side.at[plane], side_send.at[0], side_recv.at[plane], band=outer)

    def relay(plane):
        return remote(other.at[plane], other.at[plane], relay_send.at[0], other_recv.at[plane], band=outer)

    @pl.loop(0, planes)
    def _(plane):
        total = jnp.zeros((rows, lanes), jnp.float32)
        for index in range(norb):
            cells = orbs[index, plane]
            total = total + share[index] * cells * cells

        @pl.when(has_outer)
        def _():
            own[plane] = total

        @pl.when(jnp.logical_not(has_outer))
        def _():
            acc[plane] = total

            @pl.when(is_mid)
            def _():
                cross(plane).start()

            @pl.when(jnp.logical_not(is_mid))
            def _():
                to_inner(plane).start()


    @pl.loop(0, extent)
    def _(index):
        clear_rows(eps, index)
        for turn in range(ITERS):
            clear_rows(fields.at[turn], index)

    @pl.when(jnp.logical_not(has_left))
    def _():
        for index in range(ITERS):
            eps[index, body, :] = jnp.zeros((rows, lanes), jnp.float32)
            fields[0, index, body, :] = jnp.zeros((rows, lanes), jnp.float32)
        for index in range(ITERS - 1):
            density[index] = jnp.zeros((rows, lanes), jnp.float32)

    @pl.when(jnp.logical_not(has_right))
    def _():
        for index in range(ITERS):
            eps[ITERS + planes + index, body, :] = jnp.zeros((rows, lanes), jnp.float32)
            fields[0, ITERS + planes + index, body, :] = jnp.zeros((rows, lanes), jnp.float32)
        for index in range(ITERS - 1):
            density[ITERS - 1 + planes + index] = jnp.zeros((rows, lanes), jnp.float32)

    for ref in [stack.at[index] for stack in (wave, *later) for index in range(per)]:
        for index in range(reach):
            clear_plane(ref, index)
            clear_plane(ref, reach + tall + index)

        @pl.loop(reach, reach + tall)
        def _(index, ref=ref):
            clear_rows(ref, index)

    gap = jnp.abs(
        lax.broadcasted_iota(jnp.int32, (2 * lanes, lanes), 0) % lanes
        - lax.broadcasted_iota(jnp.int32, (2 * lanes, lanes), 1)
    )
    weight = jnp.where(gap == 1, 135.0, jnp.where(gap == 2, -13.5, jnp.where(gap == 3, 1.0, 0.0)))
    stripes[...] = weight.astype(jnp.bfloat16)
    scale = -coeff_three / half_value

    @pl.when(has_outer)
    def _():
        @pl.loop(0, planes)
        def _(plane):
            to_inner(plane).wait_recv()
            acc[plane] = own[plane] + part_in[plane]

            @pl.when(is_mid)
            def _():
                cross(plane).start()
                back(plane, acc).start()

            @pl.when(jnp.logical_not(is_mid))
            def _():
                to_inner(plane).start()

    def settle():
        loads[1].wait()
        loads[2].wait()
        loads[3].wait()
        sides(False)
        lane = lax.broadcasted_iota(jnp.int32, (rows, lanes), 1)
        row = lax.broadcasted_iota(jnp.int32, (rows, lanes), 0)
        zero = jnp.zeros((rows, lanes), jnp.float32)

        @pl.loop(0, half + 2 * depth)
        def _(spot):
            index = 1 + shift + spot
            here = eps[index, body, :]
            ahead = jnp.where(lane < lanes - 1, pltpu.roll(here, lanes - 1, 1), zero)
            behind = jnp.where(lane > 0, pltpu.roll(here, 1, 1), zero)
            faces = (
                0.5 * (here + eps[index + 1, body, :]),
                0.5 * (here + eps[index - 1, body, :]),
                0.5 * (here + eps[index, wide + 1 : wide + 1 + rows, :]),
                0.5 * (here + eps[index, wide - 1 : wide - 1 + rows, :]),
                0.5 * (here + ahead),
                0.5 * (here + behind),
            )
            denominator = faces[0] + faces[1] + faces[2] + faces[3] + faces[4] + faces[5]
            cell = dom * planes + index - ITERS
            inside = jnp.logical_and(cell >= 0, cell < tall)
            factor = jnp.where(inside, 1.0 / jnp.where(inside, denominator, 1.0), zero)
            inverse[index] = 4.0 * factor
            for face in range(4):
                weights[face, index] = faces[face] * factor
            weights[4, index] = jnp.where(lane < lanes - 1, faces[4] * factor, zero)
            weights[5, index] = jnp.where(lane > 0, faces[5] * factor, zero)

    pl.when(jnp.logical_not(is_mid))(settle)

    @pl.loop(0, planes)
    def _(plane):
        @pl.when(jnp.logical_not(is_mid))
        def _():
            back(plane, side).wait_recv()

            @pl.when(has_outer)
            def _():
                back(plane, side).start()

        cross(plane).wait_recv()

        @pl.when(has_outer)
        def _():
            relay(plane).start()

        @pl.when(is_mid)
        def _():
            density[depth + plane] = acc[plane] + other[plane]

        @pl.when(jnp.logical_not(is_mid))
        def _():
            density[depth + plane] = side[plane] + other[plane]

        @pl.when(jnp.logical_and(jnp.logical_and(odd == 0, has_right), plane >= planes - depth))
        def _():
            den(plane, True).start()

        @pl.when(jnp.logical_and(jnp.logical_and(odd == 1, has_left), plane < depth))
        def _():
            den(plane, False).start()

    pl.when(is_mid)(settle)

    @pl.when(held)
    def _():
        feed(FEEDS[0], FEEDS[1])

    def sweep_at(turn, index):
        before, after = fields.at[turn], fields.at[turn + 1]
        here = before[index, body, :]
        total = density[index - 1] * inverse[index]
        total = total + (
            weights[0, index] * before[index + 1, body, :] + weights[1, index] * before[index - 1, body, :]
        )
        total = total + (
            weights[2, index] * before[index, wide + 1 : wide + 1 + rows, :]
            + weights[3, index] * before[index, wide - 1 : wide - 1 + rows, :]
        )
        total = total + (
            weights[4, index] * pltpu.roll(here, lanes - 1, 1) + weights[5, index] * pltpu.roll(here, 1, 1)
        )
        after[index, body, :] = total

    for turn in range(ITERS - 1):
        first = turn + jnp.where(odd == 0, ITERS, 1 + half)
        for spot in range(half + depth - 2 * turn):
            sweep_at(turn, first + spot)

    @pl.when(jnp.logical_and(odd == 0, has_left))
    def _():
        for spot in range(depth):
            den(planes - depth + spot, True).wait_recv()

    @pl.when(jnp.logical_and(odd == 1, has_right))
    def _():
        for spot in range(depth):
            den(spot, False).wait_recv()

    for turn in range(ITERS - 1):
        first = jnp.where(odd == 0, 1 + turn, ITERS + planes - turn)
        for spot in range(depth):
            sweep_at(turn, first + spot)

    def potential_at(plane):
        sweep_at(ITERS - 1, ITERS + plane)
        cells = density[depth + plane] + core[plane]
        root = jnp.exp(jnp.log(cells) * (1.0 / 3.0))
        root = root - (root - cells / (root * root)) * (1.0 / 3.0)
        pot = fields[ITERS, ITERS + plane, body, :] + slater * root
        pot_own[plane] = pot
        strength[dom * planes + plane] = (pot - (center_value + 1.5 * coeff_zero)) * (2.0 / half_value)

    mine = pl.ds(dom * planes, planes)

    def piece(step, which):
        return pl.ds(lax.rem(dom + count_dom - 2 * step, count_dom) * planes + which * half, half)

    near = jnp.where(lax.rem(dom // 2, 2) == 0, chips - 1, 1)
    order = [near] + [2 * pair for pair in range(1, chips // 2)]
    order += [lax.rem(near + 2 * pair, chips) for pair in range(1, chips // 2)]

    def spread(step):
        here = strength.at[piece(0, odd)]
        return remote(here, here, pot_send.at[0], pot_recv.at[step], dom=peer(2 * step))

    def share_pot():
        here = pot_own.at[pl.ds(shift, half)]
        return remote(here, here, mate_send.at[0], mate_recv.at[0], band=mate)

    def swap(step):
        here = strength.at[piece(step, odd)]
        return remote(here, here, swap_send.at[0], swap_recv.at[step], band=mate)

    def hand(step, late):
        here = strength.at[piece(step, 1 - odd if late else odd)]
        return remote(here, here, pass_send.at[0], pass_recv.at[step, late], dom=partner)

    @pl.loop(0, half)
    def _(spot):
        potential_at(shift + spot)

    for step in order:
        spread(chips - step).start()
    swap(0).start()
    hand(0, 0).start()
    share_pot().start()
    feed(FEEDS[1], FEEDS[2])

    def pass_on(step):
        spread(step).wait_recv()
        swap(step).start()
        hand(step, 0).start()

    for step in order[: chips // 2]:
        pass_on(step)
    swap(0).wait_recv()
    hand(0, 1).start()
    feed(FEEDS[2], len(bulk))
    for step in order[chips // 2 :]:
        pass_on(step)

    units = tall // reach
    parts = planes // reach
    span = 2 * parts
    origin = (dom // 2) * span

    levels = (wave, *later)

    def place(level, tick):
        spot = jnp.maximum(tick - 3 * level, 0)
        return jnp.minimum(spot // units, per - 1), lax.rem(origin + level + spot, units)

    def advance(tick):
        places = [place(level, tick) for level in range(DEGREE)]
        sources = [levels[level].at[places[level][0]] for level in range(DEGREE)]
        cells = jnp.concatenate(
            [
                sources[level][pl.ds(reach + places[level][1] * reach, reach), body, :].reshape(reach * rows, lanes)
                for level in range(DEGREE)
            ],
            axis=0,
        )
        high = cells.astype(jnp.bfloat16)
        rest = cells - high.astype(jnp.float32)
        mid = rest.astype(jnp.bfloat16)
        low = (rest - mid.astype(jnp.float32)).astype(jnp.bfloat16)
        lines = jnp.dot(
            jnp.concatenate([high, mid], axis=1), stripes[...], preferred_element_type=jnp.float32
        ) + jnp.dot(low, stripes[:lanes], preferred_element_type=jnp.float32)
        sums[...] = lines.reshape(DEGREE, reach, rows, lanes)
        for level in reversed(range(DEGREE)):
            index, unit = places[level]
            ref = sources[level]
            for local_plane in range(reach):
                at = unit * reach + local_plane
                here = ref[reach + at, body, :]

                def around(dist):
                    along = ref[reach + at + dist, body, :] + ref[reach + at - dist, body, :]
                    return along + (
                        ref[reach + at, wide + dist : wide + dist + rows, :]
                        + ref[reach + at, wide - dist : wide - dist + rows, :]
                    )

                total = sums[level, local_plane] + around(3)
                total = total + 135.0 * around(1) - 13.5 * around(2)
                value = strength[at] * here + scale * total
                if level == 0:
                    value = 0.5 * value
                else:
                    value = value - levels[level - 1][index, reach + at, body, :]
                if level < DEGREE - 1:
                    levels[level + 1][index, reach + at, body, :] = value
                else:
                    result[index, at] = value

    def leave(index, unit):
        block = unit // parts
        step = lax.rem(block - dom + count_dom, count_dom)
        part = lax.rem(unit, parts)
        here = result.at[index, pl.ds(unit * reach, reach)]
        there = filtered_ref.at[dom * per + index, pl.ds(part * reach, reach)]
        away = remote(here, there, out_send.at[index], out_recv.at[index], dom=block)
        return step, away, pltpu.make_async_copy(here, there, end_sem.at[1 + index * parts + part])

    hand(0, 0).wait_recv()
    hand(0, 1).wait_recv()

    @pl.loop(0, per * units + 3 * (DEGREE - 1))
    def _(tick):
        @pl.when(jnp.logical_and(lax.rem(tick, units) == 0, tick < per * units))
        def _():
            index = tick // units
            pltpu.make_async_copy(
                orbitals_ref.at[dom * per + index],
                wave.at[index, pl.ds(reach + dom * planes, planes), body],
                load_sem.at[4 + index],
            ).wait()
            arrived(index, in_send, in_recv).wait_recv()

        for ahead in range(1, chips):
            @pl.when(tick == ahead * span - SWAP_AHEAD)
            def _(step=chips - ahead):
                swap(step).wait_recv()
                hand(step, 1).start()

            @pl.when(tick == ahead * span)
            def _(step=chips - ahead):
                hand(step, 0).wait_recv()
                hand(step, 1).wait_recv()

        advance(tick)

        @pl.when(tick >= 3 * (DEGREE - 1))
        def _():
            step, away, home = leave(*place(DEGREE - 1, tick))

            @pl.when(step > 0)
            def _():
                away.start()

            @pl.when(step == 0)
            def _():
                home.start()

    share_pot().wait()
    keep = pltpu.make_async_copy(pot_own, potential_ref, end_sem.at[0])
    keep.start()
    def gone(sent, send):
        pltpu.make_async_copy(sent, sent, send).wait()

    gone(strength.at[pl.ds(0, (chips - 1) * half)], pot_send.at[0])
    gone(strength.at[pl.ds(0, chips * half)], swap_send.at[0])
    gone(strength.at[pl.ds(0, chips * planes)], pass_send.at[0])
    for index in range(per):
        arrived(index, in_send, in_recv).wait_send()

    @pl.when(is_mid)
    def _():
        gone(acc, other_send.at[0])

    @pl.when(jnp.logical_not(is_mid))
    def _():
        gone(acc, acc_send.at[0])

    @pl.when(has_outer)
    def _():
        gone(acc, side_send.at[0])
        gone(acc, relay_send.at[0])

    @pl.when(jnp.logical_and(odd == 0, has_right))
    def _():
        gone(density.at[pl.ds(0, depth)], den_send.at[0])

    @pl.when(jnp.logical_and(odd == 1, has_left))
    def _():
        gone(density.at[pl.ds(0, depth)], den_send.at[1])

    keep.wait()
    for index in range(per):
        for part in range(parts):
            leave(index, dom * parts + part)[2].wait()
        arrived(index, out_send, out_recv).wait()


def deliver(direct, held_pot, held_filtered, potential_ref, filtered_ref, buf, pot_buf, in_sem, out_sem):
    norb = held_filtered.shape[0]
    if direct:
        puts = [pltpu.make_async_copy(held_pot, potential_ref, out_sem.at[norb])]
        puts += [pltpu.make_async_copy(held_filtered.at[i], filtered_ref.at[i], out_sem.at[i]) for i in range(norb)]
        for put in puts:
            put.start()
    else:
        gets = [pltpu.make_async_copy(held_pot, pot_buf, in_sem.at[norb])]
        gets += [pltpu.make_async_copy(held_filtered.at[i], buf.at[i], in_sem.at[i]) for i in range(norb)]
        puts = [pltpu.make_async_copy(pot_buf, potential_ref, out_sem.at[norb])]
        puts += [pltpu.make_async_copy(buf.at[i], filtered_ref.at[i], out_sem.at[i]) for i in range(norb)]
        for get in gets:
            get.start()
        for get, put in zip(gets, puts):
            get.wait()
            put.start()
    for put in puts:
        put.wait()


def fast(count_band, count_dom, orbitals, occupation, dielectric, core_density, start_field):
    norb, planes, rows, lanes = orbitals.shape
    per = norb // count_dom
    tall = count_dom * planes
    extent = planes + 2 * ITERS
    high = rows + 16
    chips = count_dom // 2

    def vmem(*shape):
        return pltpu.VMEM(shape, jnp.float32)

    def dma(*shape):
        return pltpu.SemaphoreType.DMA(shape)

    parts = planes // 3
    scratch = [
        vmem(norb, planes, rows, lanes),
        pltpu.SMEM((norb,), jnp.float32),
        vmem(planes, rows, lanes),
        vmem(planes, rows, lanes),
        vmem(planes, rows, lanes),
        vmem(planes, rows, lanes),
        vmem(planes, rows, lanes),
        vmem(planes + 2 * (ITERS - 1), rows, lanes),
        vmem(extent, high, lanes),
        vmem(ITERS + 1, extent, high, lanes),
        vmem(6, extent, rows, lanes),
        vmem(extent, rows, lanes),
        vmem(planes, rows, lanes),
        vmem(planes, rows, lanes),
        vmem(tall, rows, lanes),
        vmem(per, tall + 6, high, lanes),
        vmem(per, tall + 6, high, lanes),
        vmem(per, tall + 6, high, lanes),
        vmem(per, tall + 6, high, lanes),
        vmem(per, tall, rows, lanes),
        pltpu.VMEM((2 * lanes, lanes), jnp.bfloat16),
        vmem(DEGREE, 3, rows, lanes),
        dma(4 + per),
        dma(1),
        dma(4), dma(4),
        dma(per), dma(per),
        dma(1), dma(planes),
        dma(1), dma(planes),
        dma(1), dma(planes),
        dma(1),
        dma(2), dma(2, ITERS - 1),
        dma(1), dma(chips),
        dma(1), dma(chips),
        dma(1), dma(1),
        dma(1), dma(chips, 2),
        dma(per), dma(per),
        dma(1 + per * parts),
    ]

    def kernel(*refs):
        exchange(count_band, count_dom, refs[:5], refs[5], refs[6], refs[7:])

    hbm = pl.BlockSpec(memory_space=pl.ANY)

    def pin(array):
        return pltpu.with_memory_space_constraint(array, pltpu.HBM)

    held = pl.pallas_call(
        kernel,
        out_shape=(
            jax.ShapeDtypeStruct((planes, rows, lanes), jnp.float32),
            jax.ShapeDtypeStruct(orbitals.shape, jnp.float32),
        ),
        in_specs=[hbm] * 5,
        out_specs=(hbm, hbm),
        scratch_shapes=scratch,
        compiler_params=pltpu.CompilerParams(
            collective_id=0, has_side_effects=True, vmem_limit_bytes=40 * 1024 * 1024
        ),
        name="filter_whole",
    )(pin(orbitals), pin(occupation), pin(dielectric), pin(core_density), pin(start_field))
    hold = (planes, rows, lanes) if not True else (8, 8, 128)
    return pl.pallas_call(
        functools.partial(deliver, True),
        out_shape=(
            jax.ShapeDtypeStruct((planes, rows, lanes), jnp.float32),
            jax.ShapeDtypeStruct(orbitals.shape, jnp.float32),
        ),
        in_specs=[hbm, hbm],
        out_specs=(hbm, hbm),
        scratch_shapes=[vmem(norb, *hold), vmem(*hold), dma(norb + 1), dma(norb + 1)],
        compiler_params=pltpu.CompilerParams(vmem_limit_bytes=16 * 1024 * 1024),
        name="deliver",
    )(*held)


def program(count_band, count_dom, *arrays):
    norb, planes, rows, lanes = arrays[0].shape
    suits = (
        norb % count_dom == 0
        and count_dom % 4 == 0
        and count_dom > 2
        and count_band % 2 == 0
        and planes >= ITERS
        and planes % 6 == 0
        and rows % 8 == 0
        and lanes == 128
    )
    if suits:
        return fast(count_band, count_dom, *arrays)
    return local(*arrays)


def solution(mesh):
    return jax.shard_map(
        functools.partial(program, mesh.shape["band"], mesh.shape["dom"]),
        mesh=mesh,
        in_specs=(
            P("band", "dom", None, None),
            P("band"),
            P("dom", None, None),
            P("dom", None, None),
            P("dom", None, None),
        ),
        out_specs=(P("dom", None, None), P("band", "dom", None, None)),
        check_vma=False,
    )
```

```python
import functools

import jax
import jax.numpy as jnp
from jax import lax
from jax.experimental import pallas as pl
from jax.experimental.pallas import tpu as pltpu
from jax.sharding import PartitionSpec as P

ITERS = 4
DEGREE = 4


coeff_one = 1.5
coeff_two = -0.15
coeff_three = 1.0 / 90.0
coeff_zero = -49.0 / 18.0
center_value = 5.25
half_value = 4.75
slater = -0.9847450218426964


def padded_2(cells, sides, width):
    for axis, dim in sides:
        count = lax.axis_size(axis)
        ends = count - 1
        head = lax.slice_in_dim(cells, 0, width, axis=dim)
        tail = lax.slice_in_dim(cells, cells.shape[dim] - width, cells.shape[dim], axis=dim)
        cells = jnp.concatenate(
            [
                lax.ppermute(tail, axis, [(i, (i + 1) % count) for i in range(ends)]),
                cells,
                lax.ppermute(head, axis, [((i + 1) % count, i) for i in range(ends)]),
            ],
            axis=dim,
        )
    return cells


def laplace(padded):
    size_x = padded.shape[-3] - 6
    size_y = padded.shape[-2] - 6
    size_z = padded.shape[-1] - 6
    core = padded[..., 3 : 3 + size_x, 3 : 3 + size_y, 3 : 3 + size_z]
    total = 3.0 * coeff_zero * core
    for dist, weight in ((1, coeff_one), (2, coeff_two), (3, coeff_three)):
        along = padded[..., 3 + dist : 3 + dist + size_x, 3 : 3 + size_y, 3 : 3 + size_z]
        along = along + padded[..., 3 - dist : 3 - dist + size_x, 3 : 3 + size_y, 3 : 3 + size_z]
        along = along + padded[..., 3 : 3 + size_x, 3 + dist : 3 + dist + size_y, 3 : 3 + size_z]
        along = along + padded[..., 3 : 3 + size_x, 3 - dist : 3 - dist + size_y, 3 : 3 + size_z]
        along = along + padded[..., 3 : 3 + size_x, 3 : 3 + size_y, 3 + dist : 3 + dist + size_z]
        along = along + padded[..., 3 : 3 + size_x, 3 : 3 + size_y, 3 - dist : 3 - dist + size_z]
        total = total + weight * along
    return total


def face_weights(permit, padded):
    weights = (
        0.5 * (permit + padded[2:, 1:-1, 1:-1]),
        0.5 * (permit + padded[:-2, 1:-1, 1:-1]),
        0.5 * (permit + padded[1:-1, 2:, 1:-1]),
        0.5 * (permit + padded[1:-1, :-2, 1:-1]),
        0.5 * (permit + padded[1:-1, 1:-1, 2:]),
        0.5 * (permit + padded[1:-1, 1:-1, :-2]),
    )
    denominator = weights[0] + weights[1] + weights[2] + weights[3] + weights[4] + weights[5]
    return (weights, denominator)


def sweep(padded, weights, denominator, source):
    numerator = weights[0] * padded[2:, 1:-1, 1:-1] + weights[1] * padded[:-2, 1:-1, 1:-1]
    numerator = (
        numerator + weights[2] * padded[1:-1, 2:, 1:-1] + weights[3] * padded[1:-1, :-2, 1:-1]
    )
    numerator = (
        numerator + weights[4] * padded[1:-1, 1:-1, 2:] + weights[5] * padded[1:-1, 1:-1, :-2]
    )
    return (numerator + source) / denominator


def copies_rim(block):
    padded = padded_2(block, (("dom", 0),), 1)
    return jnp.pad(padded, ((0, 0), (1, 1), (1, 1)))


def apply_extended(padded_x, pot):
    padded = jnp.pad(padded_x, ((0, 0), (0, 0), (3, 3), (3, 3)))
    inner = padded_x[:, 3:-3]
    return -0.5 * laplace(padded) + pot[None] * inner


def local(orbitals, occupation, dielectric, core_density, start_field):
    partial_density = jnp.sum(occupation[:, None, None, None] * orbitals * orbitals, axis=0)
    density = lax.psum(partial_density, "band")
    permit_pad = padded_2(dielectric, (("dom", 0),), 1)
    permit_pad = jnp.pad(permit_pad, ((0, 0), (1, 1), (1, 1)))
    weights, denominator = face_weights(dielectric, permit_pad)
    source = 4.0 * density
    field = start_field
    for turn_index in range(ITERS):
        field = sweep(copies_rim(field), weights, denominator, source)
    potential = field + slater * jnp.cbrt(density + core_density)

    def hamil(block):
        padded = padded_2(block, (("dom", 1),), 3)
        return apply_extended(padded, potential)

    before = orbitals
    current = (hamil(orbitals) - center_value * orbitals) / half_value
    for turn_index in range(DEGREE - 1):
        nextone = 2.0 * (hamil(current) - center_value * current) / half_value - before
        before = current
        current = nextone
    return (potential, current)


MESH = pl.DeviceIdType.MESH
FEEDS = (5, 6, 14)
SWAP_AHEAD = 2


def exchange(count_band, count_dom, refs_in, potential_ref, filtered_ref, scratch):
    orbitals_ref, occupation_ref, dielectric_ref, core_ref, start_ref = refs_in
    (
        orbs, share, own, part_in, side, other, acc, density, eps, fields, weights, inverse,
        core, pot_own, strength, wave, later_one, later_two, later_three, result, stripes, sums,
        load_sem, share_sem, halo_send, halo_recv, in_send, in_recv, acc_send, acc_recv,
        side_send, side_recv, other_send, other_recv, relay_send,
        den_send, den_recv, pot_send, pot_recv, swap_send, swap_recv, mate_send, mate_recv, pass_send, pass_recv, out_send, out_recv, end_sem,
    ) = scratch
    later = (later_one, later_two, later_three)
    norb, planes, rows, lanes = orbitals_ref.shape
    per = norb // count_dom
    wide = 8
    reach = 3
    band = lax.axis_index("band")
    dom = lax.axis_index("dom")
    middle = count_band // 2
    in_left = band < middle
    toward = jnp.where(in_left, 1, -1)
    inner = band + toward
    outer = band - toward
    has_outer = jnp.logical_and(band > 0, band < count_band - 1)
    is_mid = jnp.logical_or(band == middle - 1, band == middle)
    has_left = dom > 0
    has_right = dom < count_dom - 1
    partner = dom + 1 - 2 * lax.rem(dom, 2)
    body = pl.ds(wide, rows)
    half = planes // 2
    chips = count_dom // 2
    odd = lax.rem(band, 2)
    mate = band + 1 - 2 * odd
    shift = odd * half

    def peer(step):
        return lax.rem(dom + step, count_dom)

    def remote(src, dst, send, recv, **where):
        return pltpu.make_async_remote_copy(
            src_ref=src, dst_ref=dst, send_sem=send, recv_sem=recv, device_id=where, device_id_type=MESH
        )

    loads = [
        pltpu.make_async_copy(orbitals_ref, orbs, load_sem.at[0]),
        pltpu.make_async_copy(dielectric_ref, eps.at[pl.ds(ITERS, planes), body], load_sem.at[1]),
        pltpu.make_async_copy(start_ref, fields.at[0, pl.ds(ITERS, planes), body], load_sem.at[2]),
        pltpu.make_async_copy(core_ref, core, load_sem.at[3]),
    ]
    for index in range(per):
        loads.append(
            pltpu.make_async_copy(
                orbitals_ref.at[dom * per + index],
                wave.at[index, pl.ds(reach + dom * planes, planes), body],
                load_sem.at[4 + index],
            )
        )
    barrier = pltpu.get_barrier_semaphore()
    for step in range(1, count_dom):
        pl.semaphore_signal(barrier, inc=1, device_id={"dom": peer(step)}, device_id_type=MESH)
    pl.semaphore_signal(barrier, inc=1, device_id={"band": inner}, device_id_type=MESH)
    pl.semaphore_signal(barrier, inc=1, device_id={"band": band + 1 - 2 * lax.rem(band, 2)}, device_id_type=MESH)

    @pl.when(has_outer)
    def _():
        pl.semaphore_signal(barrier, inc=1, device_id={"band": outer}, device_id_type=MESH)

    shares = pltpu.make_async_copy(occupation_ref, share, share_sem.at[0])
    shares.start()
    for copy in loads:
        copy.start()

    def clear_rows(ref, index):
        ref[index, :wide, :] = jnp.zeros((wide, lanes), jnp.float32)
        ref[index, wide + rows :, :] = jnp.zeros((wide, lanes), jnp.float32)

    def clear_plane(ref, index):
        ref[index] = jnp.zeros(ref.shape[1:], jnp.float32)

    extent = planes + 2 * ITERS
    tall = count_dom * planes
    pl.semaphore_wait(barrier, count_dom + 1 + jnp.where(has_outer, 1, 0))

    reserve = max(ITERS - half, 1)

    def halo(source, target, index, deep_left):
        from_left, from_right = (ITERS, reserve) if deep_left else (reserve, ITERS)
        right = remote(
            source.at[pl.ds(planes - from_left, from_left)], target.at[pl.ds(ITERS - from_left, from_left), body],
            halo_send.at[index], halo_recv.at[index], dom=dom + 1,
        )
        left = remote(
            source.at[pl.ds(0, from_right)], target.at[pl.ds(ITERS + planes, from_right), body],
            halo_send.at[index + 1], halo_recv.at[index + 1], dom=dom - 1,
        )
        return right, left

    depth = ITERS - 1

    def den(plane, right):
        spot = plane - (planes - depth) if right else plane
        here = density.at[depth + plane]
        there = density.at[spot] if right else density.at[depth + planes + spot]
        way = 0 if right else 1
        return remote(
            here, there, den_send.at[way], den_recv.at[way, spot], dom=dom + 1 if right else dom - 1
        )

    def sides(start):
        for parity in range(2):
            for here, mine, theirs in ((has_right, 0, 1), (has_left, 1, 0)):
                @pl.when(jnp.logical_and(odd == parity, here))
                def _(parity=parity, mine=mine, theirs=theirs):
                    for source, target, index in ((dielectric_ref, eps, 0), (start_ref, fields.at[0], 2)):
                        pair = halo(source, target, index, parity == 0)
                        if start:
                            pair[mine].start()
                        else:
                            pair[mine].wait_send()
                            pair[theirs].wait_recv()

    sides(True)

    def incoming(index, step):
        return remote(
            orbitals_ref.at[peer(step) * per + index],
            wave.at[index, pl.ds(reach + dom * planes, planes), body],
            in_send.at[index], in_recv.at[index], dom=peer(step),
        )

    def arrived(index, send, recv):
        here = result.at[index, pl.ds(0, tall - planes)]
        return remote(here, wave.at[index, pl.ds(reach, tall - planes), body], send.at[index], recv.at[index], dom=partner)

    bulk = [(index, step) for index in range(per) for step in range(1, count_dom)]

    def feed(start, stop):
        for index, step in bulk[start:stop]:
            incoming(index, step).start()

    held = jnp.logical_and(lax.rem(dom + band, 2) == 1, jnp.where(odd == 0, dom < count_dom - 1, dom > 0))
    feed(0, FEEDS[0])

    @pl.when(jnp.logical_not(held))
    def _():
        feed(FEEDS[0], FEEDS[1])

    shares.wait()
    loads[0].wait()

    def to_inner(plane):
        return remote(acc.at[plane], part_in.at[plane], acc_send.at[0], acc_recv.at[plane], band=inner)

    def cross(plane):
        return remote(acc.at[plane], other.at[plane], other_send.at[0], other_recv.at[plane], band=inner)

    def back(plane, source):
        return remote(source.at[plane], side.at[plane], side_send.at[0], side_recv.at[plane], band=outer)

    def relay(plane):
        return remote(other.at[plane], other.at[plane], relay_send.at[0], other_recv.at[plane], band=outer)

    @pl.loop(0, planes)
    def _(plane):
        total = jnp.zeros((rows, lanes), jnp.float32)
        for index in range(norb):
            cells = orbs[index, plane]
            total = total + share[index] * cells * cells

        @pl.when(has_outer)
        def _():
            own[plane] = total

        @pl.when(jnp.logical_not(has_outer))
        def _():
            acc[plane] = total

            @pl.when(is_mid)
            def _():
                cross(plane).start()

            @pl.when(jnp.logical_not(is_mid))
            def _():
                to_inner(plane).start()


    @pl.loop(0, extent)
    def _(index):
        clear_rows(eps, index)
        for turn in range(ITERS):
            clear_rows(fields.at[turn], index)

    @pl.when(jnp.logical_not(has_left))
    def _():
        for index in range(ITERS):
            eps[index, body, :] = jnp.zeros((rows, lanes), jnp.float32)
            fields[0, index, body, :] = jnp.zeros((rows, lanes), jnp.float32)
        for index in range(ITERS - 1):
            density[index] = jnp.zeros((rows, lanes), jnp.float32)

    @pl.when(jnp.logical_not(has_right))
    def _():
        for index in range(ITERS):
            eps[ITERS + planes + index, body, :] = jnp.zeros((rows, lanes), jnp.float32)
            fields[0, ITERS + planes + index, body, :] = jnp.zeros((rows, lanes), jnp.float32)
        for index in range(ITERS - 1):
            density[ITERS - 1 + planes + index] = jnp.zeros((rows, lanes), jnp.float32)

    for ref in [stack.at[index] for stack in (wave, *later) for index in range(per)]:
        for index in range(reach):
            clear_plane(ref, index)
            clear_plane(ref, reach + tall + index)

        @pl.loop(reach, reach + tall)
        def _(index, ref=ref):
            clear_rows(ref, index)

    gap = jnp.abs(
        lax.broadcasted_iota(jnp.int32, (2 * lanes, lanes), 0) % lanes
        - lax.broadcasted_iota(jnp.int32, (2 * lanes, lanes), 1)
    )
    weight = jnp.where(gap == 1, 135.0, jnp.where(gap == 2, -13.5, jnp.where(gap == 3, 1.0, 0.0)))
    stripes[...] = weight.astype(jnp.bfloat16)
    scale = -coeff_three / half_value

    @pl.when(has_outer)
    def _():
        @pl.loop(0, planes)
        def _(plane):
            to_inner(plane).wait_recv()
            acc[plane] = own[plane] + part_in[plane]

            @pl.when(is_mid)
            def _():
                cross(plane).start()
                back(plane, acc).start()

            @pl.when(jnp.logical_not(is_mid))
            def _():
                to_inner(plane).start()

    def settle():
        loads[1].wait()
        loads[2].wait()
        loads[3].wait()
        sides(False)
        lane = lax.broadcasted_iota(jnp.int32, (rows, lanes), 1)
        row = lax.broadcasted_iota(jnp.int32, (rows, lanes), 0)
        zero = jnp.zeros((rows, lanes), jnp.float32)

        @pl.loop(0, half + 2 * depth)
        def _(spot):
            index = 1 + shift + spot
            here = eps[index, body, :]
            ahead = jnp.where(lane < lanes - 1, pltpu.roll(here, lanes - 1, 1), zero)
            behind = jnp.where(lane > 0, pltpu.roll(here, 1, 1), zero)
            faces = (
                0.5 * (here + eps[index + 1, body, :]),
                0.5 * (here + eps[index - 1, body, :]),
                0.5 * (here + eps[index, wide + 1 : wide + 1 + rows, :]),
                0.5 * (here + eps[index, wide - 1 : wide - 1 + rows, :]),
                0.5 * (here + ahead),
                0.5 * (here + behind),
            )
            denominator = faces[0] + faces[1] + faces[2] + faces[3] + faces[4] + faces[5]
            cell = dom * planes + index - ITERS
            inside = jnp.logical_and(cell >= 0, cell < tall)
            factor = jnp.where(inside, 1.0 / jnp.where(inside, denominator, 1.0), zero)
            inverse[index] = 4.0 * factor
            for face in range(4):
                weights[face, index] = faces[face] * factor
            weights[4, index] = jnp.where(lane < lanes - 1, faces[4] * factor, zero)
            weights[5, index] = jnp.where(lane > 0, faces[5] * factor, zero)

    pl.when(jnp.logical_not(is_mid))(settle)

    @pl.loop(0, planes)
    def _(plane):
        @pl.when(jnp.logical_not(is_mid))
        def _():
            back(plane, side).wait_recv()

            @pl.when(has_outer)
            def _():
                back(plane, side).start()

        cross(plane).wait_recv()

        @pl.when(has_outer)
        def _():
            relay(plane).start()

        @pl.when(is_mid)
        def _():
            density[depth + plane] = acc[plane] + other[plane]

        @pl.when(jnp.logical_not(is_mid))
        def _():
            density[depth + plane] = side[plane] + other[plane]

        @pl.when(jnp.logical_and(jnp.logical_and(odd == 0, has_right), plane >= planes - depth))
        def _():
            den(plane, True).start()

        @pl.when(jnp.logical_and(jnp.logical_and(odd == 1, has_left), plane < depth))
        def _():
            den(plane, False).start()

    pl.when(is_mid)(settle)

    @pl.when(held)
    def _():
        feed(FEEDS[0], FEEDS[1])

    def sweep_at(turn, index):
        before, after = fields.at[turn], fields.at[turn + 1]
        here = before[index, body, :]
        total = density[index - 1] * inverse[index]
        total = total + (
            weights[0, index] * before[index + 1, body, :] + weights[1, index] * before[index - 1, body, :]
        )
        total = total + (
            weights[2, index] * before[index, wide + 1 : wide + 1 + rows, :]
            + weights[3, index] * before[index, wide - 1 : wide - 1 + rows, :]
        )
        total = total + (
            weights[4, index] * pltpu.roll(here, lanes - 1, 1) + weights[5, index] * pltpu.roll(here, 1, 1)
        )
        after[index, body, :] = total

    for turn in range(ITERS - 1):
        first = turn + jnp.where(odd == 0, ITERS, 1 + half)
        for spot in range(half + depth - 2 * turn):
            sweep_at(turn, first + spot)

    @pl.when(jnp.logical_and(odd == 0, has_left))
    def _():
        for spot in range(depth):
            den(planes - depth + spot, True).wait_recv()

    @pl.when(jnp.logical_and(odd == 1, has_right))
    def _():
        for spot in range(depth):
            den(spot, False).wait_recv()

    for turn in range(ITERS - 1):
        first = jnp.where(odd == 0, 1 + turn, ITERS + planes - turn)
        for spot in range(depth):
            sweep_at(turn, first + spot)

    def potential_at(plane):
        sweep_at(ITERS - 1, ITERS + plane)
        cells = density[depth + plane] + core[plane]
        root = jnp.exp(jnp.log(cells) * (1.0 / 3.0))
        root = root - (root - cells / (root * root)) * (1.0 / 3.0)
        pot = fields[ITERS, ITERS + plane, body, :] + slater * root
        pot_own[plane] = pot
        strength[dom * planes + plane] = (pot - (center_value + 1.5 * coeff_zero)) * (2.0 / half_value)

    mine = pl.ds(dom * planes, planes)

    def piece(step, which):
        return pl.ds(lax.rem(dom + count_dom - 2 * step, count_dom) * planes + which * half, half)

    near = jnp.where(lax.rem(dom // 2, 2) == 0, chips - 1, 1)
    order = [near] + [2 * pair for pair in range(1, chips // 2)]
    order += [lax.rem(near + 2 * pair, chips) for pair in range(1, chips // 2)]

    def spread(step):
        here = strength.at[piece(0, odd)]
        return remote(here, here, pot_send.at[0], pot_recv.at[step], dom=peer(2 * step))

    def share_pot():
        here = pot_own.at[pl.ds(shift, half)]
        return remote(here, here, mate_send.at[0], mate_recv.at[0], band=mate)

    def swap(step):
        here = strength.at[piece(step, odd)]
        return remote(here, here, swap_send.at[0], swap_recv.at[step], band=mate)

    def hand(step, late):
        here = strength.at[piece(step, 1 - odd if late else odd)]
        return remote(here, here, pass_send.at[0], pass_recv.at[step, late], dom=partner)

    @pl.loop(0, half)
    def _(spot):
        potential_at(shift + spot)

    for step in order:
        spread(chips - step).start()
    swap(0).start()
    hand(0, 0).start()
    share_pot().start()
    feed(FEEDS[1], FEEDS[2])

    def pass_on(step):
        spread(step).wait_recv()
        swap(step).start()
        hand(step, 0).start()

    for step in order[: chips // 2]:
        pass_on(step)
    swap(0).wait_recv()
    hand(0, 1).start()
    feed(FEEDS[2], len(bulk))
    for step in order[chips // 2 :]:
        pass_on(step)

    units = tall // reach
    parts = planes // reach
    span = 2 * parts
    origin = (dom // 2) * span

    levels = (wave, *later)

    def place(level, tick):
        spot = jnp.maximum(tick - 3 * level, 0)
        return jnp.minimum(spot // units, per - 1), lax.rem(origin + level + spot, units)

    def advance(tick):
        places = [place(level, tick) for level in range(DEGREE)]
        sources = [levels[level].at[places[level][0]] for level in range(DEGREE)]
        cells = jnp.concatenate(
            [
                sources[level][pl.ds(reach + places[level][1] * reach, reach), body, :].reshape(reach * rows, lanes)
                for level in range(DEGREE)
            ],
            axis=0,
        )
        high = cells.astype(jnp.bfloat16)
        rest = cells - high.astype(jnp.float32)
        mid = rest.astype(jnp.bfloat16)
        low = (rest - mid.astype(jnp.float32)).astype(jnp.bfloat16)
        lines = jnp.dot(
            jnp.concatenate([high, mid], axis=1), stripes[...], preferred_element_type=jnp.float32
        ) + jnp.dot(low, stripes[:lanes], preferred_element_type=jnp.float32)
        sums[...] = lines.reshape(DEGREE, reach, rows, lanes)
        for level in reversed(range(DEGREE)):
            index, unit = places[level]
            ref = sources[level]
            for local_plane in range(reach):
                at = unit * reach + local_plane
                here = ref[reach + at, body, :]

                def around(dist):
                    along = ref[reach + at + dist, body, :] + ref[reach + at - dist, body, :]
                    return along + (
                        ref[reach + at, wide + dist : wide + dist + rows, :]
                        + ref[reach + at, wide - dist : wide - dist + rows, :]
                    )

                total = sums[level, local_plane] + around(3)
                total = total + 135.0 * around(1) - 13.5 * around(2)
                value = strength[at] * here + scale * total
                if level == 0:
                    value = 0.5 * value
                else:
                    value = value - levels[level - 1][index, reach + at, body, :]
                if level < DEGREE - 1:
                    levels[level + 1][index, reach + at, body, :] = value
                else:
                    result[index, at] = value

    def leave(index, unit):
        block = unit // parts
        step = lax.rem(block - dom + count_dom, count_dom)
        part = lax.rem(unit, parts)
        here = result.at[index, pl.ds(unit * reach, reach)]
        there = filtered_ref.at[dom * per + index, pl.ds(part * reach, reach)]
        away = remote(here, there, out_send.at[index], out_recv.at[index], dom=block)
        return step, away, pltpu.make_async_copy(here, there, end_sem.at[1 + index * parts + part])

    hand(0, 0).wait_recv()
    hand(0, 1).wait_recv()

    @pl.loop(0, per * units + 3 * (DEGREE - 1))
    def _(tick):
        @pl.when(jnp.logical_and(lax.rem(tick, units) == 0, tick < per * units))
        def _():
            index = tick // units
            pltpu.make_async_copy(
                orbitals_ref.at[dom * per + index],
                wave.at[index, pl.ds(reach + dom * planes, planes), body],
                load_sem.at[4 + index],
            ).wait()
            arrived(index, in_send, in_recv).wait_recv()

        for ahead in range(1, chips):
            @pl.when(tick == ahead * span - SWAP_AHEAD)
            def _(step=chips - ahead):
                swap(step).wait_recv()
                hand(step, 1).start()

            @pl.when(tick == ahead * span)
            def _(step=chips - ahead):
                hand(step, 0).wait_recv()
                hand(step, 1).wait_recv()

        advance(tick)

        @pl.when(tick >= 3 * (DEGREE - 1))
        def _():
            step, away, home = leave(*place(DEGREE - 1, tick))

            @pl.when(step > 0)
            def _():
                away.start()

            @pl.when(step == 0)
            def _():
                home.start()

    share_pot().wait()
    keep = pltpu.make_async_copy(pot_own, potential_ref, end_sem.at[0])
    keep.start()
    def gone(sent, send):
        pltpu.make_async_copy(sent, sent, send).wait()

    gone(strength.at[pl.ds(0, (chips - 1) * half)], pot_send.at[0])
    gone(strength.at[pl.ds(0, chips * half)], swap_send.at[0])
    gone(strength.at[pl.ds(0, chips * planes)], pass_send.at[0])
    for index in range(per):
        arrived(index, in_send, in_recv).wait_send()

    @pl.when(is_mid)
    def _():
        gone(acc, other_send.at[0])

    @pl.when(jnp.logical_not(is_mid))
    def _():
        gone(acc, acc_send.at[0])

    @pl.when(has_outer)
    def _():
        gone(acc, side_send.at[0])
        gone(acc, relay_send.at[0])

    @pl.when(jnp.logical_and(odd == 0, has_right))
    def _():
        gone(density.at[pl.ds(0, depth)], den_send.at[0])

    @pl.when(jnp.logical_and(odd == 1, has_left))
    def _():
        gone(density.at[pl.ds(0, depth)], den_send.at[1])

    keep.wait()
    for index in range(per):
        for part in range(parts):
            leave(index, dom * parts + part)[2].wait()
        arrived(index, out_send, out_recv).wait()


def deliver(direct, held_pot, held_filtered, potential_ref, filtered_ref, buf, pot_buf, in_sem, out_sem):
    norb = held_filtered.shape[0]
    if direct:
        puts = [pltpu.make_async_copy(held_pot, potential_ref, out_sem.at[norb])]
        puts += [pltpu.make_async_copy(held_filtered.at[i], filtered_ref.at[i], out_sem.at[i]) for i in range(norb)]
        for put in puts:
            put.start()
    else:
        gets = [pltpu.make_async_copy(held_pot, pot_buf, in_sem.at[norb])]
        gets += [pltpu.make_async_copy(held_filtered.at[i], buf.at[i], in_sem.at[i]) for i in range(norb)]
        puts = [pltpu.make_async_copy(pot_buf, potential_ref, out_sem.at[norb])]
        puts += [pltpu.make_async_copy(buf.at[i], filtered_ref.at[i], out_sem.at[i]) for i in range(norb)]
        for get in gets:
            get.start()
        for get, put in zip(gets, puts):
            get.wait()
            put.start()
    for put in puts:
        put.wait()


def fast(count_band, count_dom, orbitals, occupation, dielectric, core_density, start_field):
    norb, planes, rows, lanes = orbitals.shape
    per = norb // count_dom
    tall = count_dom * planes
    extent = planes + 2 * ITERS
    high = rows + 16
    chips = count_dom // 2

    def vmem(*shape):
        return pltpu.VMEM(shape, jnp.float32)

    def dma(*shape):
        return pltpu.SemaphoreType.DMA(shape)

    parts = planes // 3
    scratch = [
        vmem(norb, planes, rows, lanes),
        pltpu.SMEM((norb,), jnp.float32),
        vmem(planes, rows, lanes),
        vmem(planes, rows, lanes),
        vmem(planes, rows, lanes),
        vmem(planes, rows, lanes),
        vmem(planes, rows, lanes),
        vmem(planes + 2 * (ITERS - 1), rows, lanes),
        vmem(extent, high, lanes),
        vmem(ITERS + 1, extent, high, lanes),
        vmem(6, extent, rows, lanes),
        vmem(extent, rows, lanes),
        vmem(planes, rows, lanes),
        vmem(planes, rows, lanes),
        vmem(tall, rows, lanes),
        vmem(per, tall + 6, high, lanes),
        vmem(per, tall + 6, high, lanes),
        vmem(per, tall + 6, high, lanes),
        vmem(per, tall + 6, high, lanes),
        vmem(per, tall, rows, lanes),
        pltpu.VMEM((2 * lanes, lanes), jnp.bfloat16),
        vmem(DEGREE, 3, rows, lanes),
        dma(4 + per),
        dma(1),
        dma(4), dma(4),
        dma(per), dma(per),
        dma(1), dma(planes),
        dma(1), dma(planes),
        dma(1), dma(planes),
        dma(1),
        dma(2), dma(2, ITERS - 1),
        dma(1), dma(chips),
        dma(1), dma(chips),
        dma(1), dma(1),
        dma(1), dma(chips, 2),
        dma(per), dma(per),
        dma(1 + per * parts),
    ]

    def kernel(*refs):
        exchange(count_band, count_dom, refs[:5], refs[5], refs[6], refs[7:])

    hbm = pl.BlockSpec(memory_space=pl.ANY)

    def pin(array):
        return pltpu.with_memory_space_constraint(array, pltpu.HBM)

    held = pl.pallas_call(
        kernel,
        out_shape=(
            jax.ShapeDtypeStruct((planes, rows, lanes), jnp.float32),
            jax.ShapeDtypeStruct(orbitals.shape, jnp.float32),
        ),
        in_specs=[hbm] * 5,
        out_specs=(hbm, hbm),
        scratch_shapes=scratch,
        compiler_params=pltpu.CompilerParams(
            collective_id=0, has_side_effects=True, vmem_limit_bytes=40 * 1024 * 1024
        ),
        name="filter_whole",
    )(pin(orbitals), pin(occupation), pin(dielectric), pin(core_density), pin(start_field))
    hold = (planes, rows, lanes) if not True else (8, 8, 128)
    return pl.pallas_call(
        functools.partial(deliver, True),
        out_shape=(
            jax.ShapeDtypeStruct((planes, rows, lanes), jnp.float32),
            jax.ShapeDtypeStruct(orbitals.shape, jnp.float32),
        ),
        in_specs=[hbm, hbm],
        out_specs=(hbm, hbm),
        scratch_shapes=[vmem(norb, *hold), vmem(*hold), dma(norb + 1), dma(norb + 1)],
        compiler_params=pltpu.CompilerParams(vmem_limit_bytes=16 * 1024 * 1024),
        name="deliver",
    )(*held)


def program(count_band, count_dom, *arrays):
    norb, planes, rows, lanes = arrays[0].shape
    suits = (
        norb % count_dom == 0
        and count_dom % 4 == 0
        and count_dom > 2
        and count_band % 2 == 0
        and planes >= ITERS
        and planes % 6 == 0
        and rows % 8 == 0
        and lanes == 128
    )
    if suits:
        return fast(count_band, count_dom, *arrays)
    return local(*arrays)


def solution(mesh):
    return jax.shard_map(
        functools.partial(program, mesh.shape["band"], mesh.shape["dom"]),
        mesh=mesh,
        in_specs=(
            P("band", "dom", None, None),
            P("band"),
            P("dom", None, None),
            P("dom", None, None),
            P("dom", None, None),
        ),
        out_specs=(P("dom", None, None), P("band", "dom", None, None)),
        check_vma=False,
    )
```
